32 devices in a mesh: dp: 8 (over y, x, core), tensor: 4 (over z).
Axes of the slice: x: 2, y: 2, z: 4, core: 2. Of those that a mesh axis runs over, the one named last changes fastest.
Arguments:
- layer_input: bfloat16 [13312, 1536], P(('dp', 'tensor')), may hold values from -6 to 6
- piece_starts: int32 [8, 2], P('dp'), may hold values from 0 to 1408, as said below
- query_weight: bfloat16 [1536, 1536], P('dp', 'tensor'), may hold values from -0.15625 to 0.15625
- key_weight: bfloat16 [1536, 1536], P('dp', 'tensor'), may hold values from -0.15625 to 0.15625
- value_weight: bfloat16 [1536, 1536], P('dp', 'tensor'), may hold values from -0.15625 to 0.15625
- out_weight: bfloat16 [1536, 1536], P('tensor', 'dp'), may hold values from -0.15625 to 0.15625
- gate_weight: bfloat16 [1536, 4096], P('dp', 'tensor'), may hold values from -0.15625 to 0.15625
- up_weight: bfloat16 [1536, 4096], P('dp', 'tensor'), may hold values from -0.15625 to 0.15625
- down_weight: bfloat16 [4096, 1536], P('tensor', 'dp'), may hold values from -0.09375 to 0.09375
- attention_gain: float32 [1536], replicated, may hold values from 0.5 to 1.5
- feedforward_gain: float32 [1536], replicated, may hold values from 0.5 to 1.5
- head_gain: float32 [1536], replicated, may hold values from 0.5 to 1.5
- score_kernel: float32 [16, 6, 11], replicated, may hold values from -1 to 1
- head_mix: float32 [8, 2, 2], replicated, may hold values from 0.3 to 1
- output_grad: bfloat16 [13312, 1536], P(('dp', 'tensor')), may hold values from -6 to 6
Outputs:
- layer_output: bfloat16 [13312, 1536], P(('dp', 'tensor'))
- input_grad: bfloat16 [13312, 1536], P(('dp', 'tensor'))
- query_grad: float32 [1536, 1536], P('dp', 'tensor')
- key_grad: float32 [1536, 1536], P('dp', 'tensor')
- value_grad: float32 [1536, 1536], P('dp', 'tensor')
- out_weight_grad: float32 [1536, 1536], P('tensor', 'dp')
- gate_grad: float32 [1536, 4096], P('dp', 'tensor')
- up_grad: float32 [1536, 4096], P('dp', 'tensor')
- down_grad: float32 [4096, 1536], P('tensor', 'dp')
- attention_gain_grad: float32 [1536], replicated
- feedforward_gain_grad: float32 [1536], replicated
- head_gain_grad: float32 [1536], replicated
- score_kernel_grad: float32 [16, 6, 11], replicated
- head_mix_grad: float32 [8, 2, 2], replicated
The draws below stay inside these ranges and needn't reach their ends.
Inputs may be any that keep to these rules, and one draw needn't show every extreme that they name: `piece_starts`: each sequence's 2 pieces of 256 tokens lie inside it, start in rising order and don't intersect.
All inputs are finite; a program needn't handle non-finite values.
Results may differ from the reference program's by a relative error of at most 0.02.
Values may be sent and summed in bfloat16 or wider, within the bound.
No kernel may reach another device: no remote copies, remote signals or barrier semaphores. Data moves between devices by JAX's collectives and lax.ppermute only.
A program may use at most 704 MiB of HBM per device.

```python
import math
import jax
import jax.numpy as jnp
from jax import lax

D = 1536
H = 16
HD = 96
FF = 4096
CQ = 6
CK = 11
LEN = 1664
PIC = 256
PICS = 2
GROUPS = 8
TOKENS = 13312


def draw_piece_starts(key, part):
    seq_total = TOKENS // LEN
    spare_room = LEN - PICS * PIC
    offsets = jax.random.randint(key, (seq_total, PICS), 0, spare_room + 1, dtype=jnp.int32)
    ordered = jnp.sort(offsets, axis=-1)
    return ordered + PIC * jnp.arange(PICS, dtype=jnp.int32)[None, :]


def shard_levels(own_key, shape, shards, smallest, top_value):
    level, own = 1.0, jax.random.fold_in(own_key, 6)
    for dim, parts in shards:
        steps = jnp.exp(jax.random.uniform(jax.random.fold_in(own, dim), (parts,), jnp.float32, smallest / len(shards), top_value / len(shards)))
        level = level * jnp.repeat(steps, shape[dim] // parts).reshape([-1 if axis == dim else 1 for axis in range(len(shape))])
    return level


def bell_draw(stream_key, shape, scale, most, cuts=(), kind=jnp.bfloat16):
    entries = scale * jax.random.normal(stream_key, shape, jnp.float32)
    if cuts:
        entries = entries * shard_levels(stream_key, shape, cuts, -0.22, 0.18)
    return jnp.clip(entries, -most, most).astype(kind)


def setup_inputs(seed: int = 0) -> dict:
    streams_of = jax.random.split(jax.random.key(seed), 16)
    return {
        "layer_input": bell_draw(streams_of[0], (TOKENS, D), 1.0, 6.0, ((0, 32),)),
        "piece_starts": draw_piece_starts(jax.random.fold_in(streams_of[15], 71), 0),
        "query_weight": bell_draw(streams_of[2], (D, D), D ** -0.5, 0.15625, ((0, 8), (1, 4))),
        "key_weight": bell_draw(streams_of[3], (D, D), D ** -0.5, 0.15625, ((0, 8), (1, 4))),
        "value_weight": bell_draw(streams_of[4], (D, D), D ** -0.5, 0.15625, ((0, 8), (1, 4))),
        "out_weight": bell_draw(streams_of[5], (D, D), D ** -0.5, 0.15625, ((0, 4), (1, 8))),
        "gate_weight": bell_draw(streams_of[6], (D, FF), D ** -0.5, 0.15625, ((0, 8), (1, 4))),
        "up_weight": bell_draw(streams_of[7], (D, FF), D ** -0.5, 0.15625, ((0, 8), (1, 4))),
        "down_weight": bell_draw(streams_of[8], (FF, D), FF ** -0.5, 0.09375, ((0, 4), (1, 8))),
        "attention_gain": jnp.clip(1.0 + 0.1 * jax.random.normal(streams_of[9], (D,), jnp.float32), 0.5, 1.5),
        "feedforward_gain": jnp.clip(1.0 + 0.1 * jax.random.normal(streams_of[10], (D,), jnp.float32), 0.5, 1.5),
        "head_gain": jnp.clip(1.0 + 0.1 * jax.random.normal(streams_of[11], (D,), jnp.float32), 0.5, 1.5),
        "score_kernel": bell_draw(streams_of[12], (H, CQ, CK), 0.2, 1.0, (), jnp.float32),
        "head_mix": jnp.clip(jax.random.uniform(streams_of[13], (GROUPS, 2, 2), jnp.float32, 0.3, 1.0), 0.3, 1.0),
        "output_grad": bell_draw(streams_of[14], (TOKENS, D), 1.0, 6.0, ((0, 32),)),
    }


HIGHEST = lax.Precision.HIGHEST
epsilon = 1e-05

@jax.custom_vjp
def low(v):
    return lax.optimization_barrier(v.astype(jnp.bfloat16)).astype(jnp.float32)

@jax.custom_vjp
def low_back(v):
    return v

def low_keep(v):
    return (low(v), None)

def low_pass(kept, grad):
    return (grad,)

def back_keep(v):
    return (v, None)

def back_low(kept, grad):
    return (low(grad),)
low.defvjp(low_keep, low_pass)
low_back.defvjp(back_keep, back_low)

def rms_norm(values, gain):
    return values * lax.rsqrt(lax.optimization_barrier(jnp.mean(values * values, axis=-1, keepdims=True)) + epsilon) * gain

def group_norm(values, gain):
    centred = values - lax.optimization_barrier(jnp.mean(values, axis=-1, keepdims=True))
    return centred * lax.rsqrt(lax.optimization_barrier(jnp.mean(centred * centred, axis=-1, keepdims=True)) + epsilon) * gain

def swiglu(gate, upper):
    return jax.nn.silu(gate) * upper

def piece_index(positions, starts):
    inside = (positions[:, None] >= starts[None, :]) & (positions[:, None] < starts[None, :] + PIC)
    labels = jnp.arange(1, starts.shape[0] + 1, dtype=jnp.int32)
    return lax.optimization_barrier(jnp.max(jnp.where(inside, labels[None, :], 0), axis=1)) - 1

def allowed_mask(positions, columns, starts):
    row_piece = piece_index(positions, starts)
    col_piece = piece_index(columns, starts)
    causal = columns[None, :] <= positions[:, None]
    shared = (row_piece[:, None] == col_piece[None, :]) & (row_piece[:, None] >= 0)
    return (causal | shared) & (positions[:, None] >= 0)

def mix_heads(probs, mixing):
    grouped = probs.reshape((mixing.shape[0], 1, 2) + probs.shape[1:])
    return lax.optimization_barrier(jnp.sum(mixing[:, :, :, None, None] * grouped, axis=2)).reshape(probs.shape)

def conv_probs(raw_scores, kernel, mixing, halo_mask, block_mask, score_scale):
    lags = kernel.shape[1]
    taps = kernel.shape[2]
    middle = taps // 2
    block_rows = block_mask.shape[0]
    length = block_mask.shape[1]
    masked = jnp.where(halo_mask[None], raw_scores * score_scale, 0.0)
    padded = jnp.pad(masked, ((0, 0), (0, 0), (middle, taps - 1 - middle)))

    def lag_step(convolved, lag_item):
        row_lag, lag_kernel = lag_item
        rows = lax.dynamic_slice_in_dim(padded, lags - 1 - row_lag, block_rows, 1)
        for key_tap in range(taps):
            window = rows[:, :, 2 * middle - key_tap:2 * middle - key_tap + length]
            convolved = convolved + lag_kernel[:, key_tap][:, None, None] * window
        return (convolved, None)
    start = jnp.zeros((raw_scores.shape[0], block_rows, length), jnp.float32)
    lag_kernels = jnp.transpose(kernel, (1, 0, 2))
    convolved, _ = lax.scan(jax.checkpoint(lag_step), start, (jnp.arange(lags, dtype=jnp.int32), lag_kernels))
    logits = jnp.where(block_mask[None], convolved, -1e+30)
    largest = lax.optimization_barrier(jnp.max(logits, axis=-1, keepdims=True))
    exponent = jnp.exp(logits - largest)
    probs = exponent / lax.optimization_barrier(jnp.sum(exponent, axis=-1, keepdims=True))
    return mix_heads(probs, mixing)

def attend(queries, key_rows, values, starts, kernel, mixing, score_scale):
    length = queries.shape[0]
    lags = kernel.shape[1]
    block_rows = length // 2
    padded = jnp.pad(queries, ((lags - 1, 0), (0, 0), (0, 0)))
    columns = jnp.arange(length, dtype=jnp.int32)

    def one_block(first_row):
        extended = lax.dynamic_slice_in_dim(padded, first_row, block_rows + lags - 1, 0)
        raw_scores = low_back(jnp.einsum('qhd,khd->hqk', extended, key_rows, precision=HIGHEST))
        positions = first_row - (lags - 1) + jnp.arange(block_rows + lags - 1, dtype=jnp.int32)
        halo_mask = allowed_mask(positions, columns, starts)
        mixed = low(conv_probs(raw_scores, kernel, mixing, halo_mask, halo_mask[lags - 1:], score_scale))
        return low_back(jnp.einsum('hqk,khd->qhd', mixed, values, precision=HIGHEST))
    firsts = jnp.arange(2, dtype=jnp.int32) * block_rows
    outputs = lax.map(jax.checkpoint(one_block), firsts)
    return outputs.reshape(queries.shape)

def layer(tokens, starts, params):
    query_weight, key_weight, value_weight, out_weight, gate_weight, up_weight, down_weight, attention_gain, feedforward_gain, head_gain, score_kernel, head_mix = params
    length = tokens.shape[0]
    normed = low(rms_norm(tokens, attention_gain))
    queries = low_back(low(jnp.dot(normed, query_weight, precision=HIGHEST)))
    key_rows = low_back(low(jnp.dot(normed, key_weight, precision=HIGHEST)))
    values = low_back(low(jnp.dot(normed, value_weight, precision=HIGHEST)))
    heads_out = attend(queries.reshape(length, H, HD), key_rows.reshape(length, H, HD), values.reshape(length, H, HD), starts, score_kernel, head_mix, 1.0 / math.sqrt(HD))
    mixed = low(group_norm(heads_out, head_gain.reshape(H, HD)))
    hidden = tokens + low_back(jnp.dot(mixed.reshape(length, D), out_weight, precision=HIGHEST))
    ffn_in = low(rms_norm(hidden, feedforward_gain))
    gate = low_back(jnp.dot(ffn_in, gate_weight, precision=HIGHEST))
    upper = low_back(jnp.dot(ffn_in, up_weight, precision=HIGHEST))
    activated = low(swiglu(gate, upper))
    return hidden + jnp.dot(activated, down_weight, precision=HIGHEST)

def reference(layer_input, piece_starts, query_weight, key_weight, value_weight, out_weight, gate_weight, up_weight, down_weight, attention_gain, feedforward_gain, head_gain, score_kernel, head_mix, output_grad):
    params = tuple((weight_in.astype(jnp.float32) for weight_in in (query_weight, key_weight, value_weight, out_weight, gate_weight, up_weight, down_weight, attention_gain, feedforward_gain, head_gain, score_kernel, head_mix)))
    tokens = layer_input.astype(jnp.float32).reshape(-1, LEN, D)
    cotangent = output_grad.astype(jnp.float32).reshape(-1, LEN, D)
    checked = jax.checkpoint(layer)

    def forward(params_in, tokens_in):
        return lax.map(lambda seq_pair: checked(seq_pair[0], seq_pair[1], params_in), (tokens_in, piece_starts))
    outputs, pullback = jax.vjp(forward, params, tokens)
    param_grads, token_grads = pullback(cotangent)
    return (outputs.reshape(-1, D).astype(jnp.bfloat16), token_grads.reshape(-1, D).astype(jnp.bfloat16), param_grads[0], param_grads[1], param_grads[2], param_grads[3], param_grads[4], param_grads[5], param_grads[6], param_grads[7], param_grads[8], param_grads[9], param_grads[10], param_grads[11])
```

```python
import functools
import math

import jax
import jax.numpy as jnp
from jax import lax
from jax.experimental import pallas as pl
from jax.experimental.pallas import tpu as pltpu
from jax.sharding import PartitionSpec as P

HD = 96
LEN = 1664
PIC = 256
TILE = 128
LANES = 128
FRONT = 64
ROWPAD = 16
VMEM_BYTES = 56 * 1024 * 1024
epsilon = 1e-05


def dot_nn(left, right):
    return jnp.dot(left, right, preferred_element_type=jnp.float32)


def dot_nt(left, right):
    return lax.dot_general(left, right, (((1,), (1,)), ((), ())), preferred_element_type=jnp.float32)


def dot_tn(left, right):
    return lax.dot_general(left, right, (((0,), (0,)), ((), ())), preferred_element_type=jnp.float32)


def row_ends(rows, starts_ref, pics):
    ends = rows
    for piece in range(pics):
        first = starts_ref[piece]
        ends = jnp.where((rows >= first) & (rows < first + PIC), first + PIC - 1, ends)
    return ends


def filter_keys(kt_ref, thi_ref, tlo_ref, kcat_ref, lags):
    for head in range(2):

        def tile_step(tile, carry):
            first = pl.multiple_of(tile * TILE, TILE)
            window = kt_ref[head, :, pl.ds(first, 2 * TILE)]
            filtered = dot_nn(window, thi_ref[head]) + dot_nn(window, tlo_ref[head])
            for lag in range(lags):
                kcat_ref[head, lag * LANES : (lag + 1) * LANES, pl.ds(first, TILE)] = filtered[
                    :, lag * TILE : (lag + 1) * TILE
                ].astype(jnp.bfloat16)
            return carry

        lax.fori_loop(0, LEN // TILE, tile_step, 0)


def lagged(rows, lags):
    return jnp.concatenate(
        [rows[ROWPAD - lag : ROWPAD - lag + TILE] for lag in range(lags)], axis=1
    ).astype(jnp.bfloat16)


def forward_kernel(
    bounds_ref, starts_ref, q_ref, kt_ref, v_ref, thi_ref, tlo_ref,
    e_ref, o_ref, inv_ref,
    kcat_ref, c_ref, qcat_ref, top_ref, sum_ref,
    *, lags, pics,
):
    block = pl.program_id(1)
    blocks = pl.num_programs(1)
    first_row = pl.multiple_of(block * TILE, TILE)

    @pl.when(block == 0)
    def _():
        filter_keys(kt_ref, thi_ref, tlo_ref, kcat_ref, lags)

    full = bounds_ref[block]
    last = bounds_ref[blocks + block]
    for head in range(2):
        rows = q_ref[head, pl.ds(first_row, TILE + ROWPAD), :].astype(jnp.float32)
        qcat_ref[head] = lagged(rows, lags)
        top_ref[head] = jnp.full((TILE, LANES), -1e30, jnp.float32)
        sum_ref[head] = jnp.zeros((TILE, LANES), jnp.float32)
        o_ref[head] = jnp.zeros(o_ref.shape[1:], jnp.float32)

    def full_tiles(first, width):
        for head in range(2):
            logits = dot_nn(qcat_ref[head], kcat_ref[head, :, pl.ds(first, width)])
            c_ref[head, :, pl.ds(first, width)] = logits
            top = top_ref[head]
            for part in range(width // LANES):
                top = jnp.maximum(top, logits[:, part * LANES : (part + 1) * LANES])
            top_ref[head] = top

    def full_step(pair, carry):
        full_tiles(pl.multiple_of(pair * 2 * TILE, 2 * TILE), 2 * TILE)
        return carry

    lax.fori_loop(0, full // 2, full_step, 0)

    @pl.when(full % 2 == 1)
    def _():
        full_tiles(pl.multiple_of((full - 1) * TILE, TILE), TILE)

    source_rows = first_row - ROWPAD + lax.broadcasted_iota(jnp.int32, (TILE + ROWPAD, 1), 0)
    source_ends = row_ends(source_rows, starts_ref, pics)
    target_rows = first_row + lax.broadcasted_iota(jnp.int32, (TILE, 1), 0)
    target_ends = row_ends(target_rows, starts_ref, pics)

    def mixed_step(tile, carry):
        first = pl.multiple_of(tile * TILE, TILE)
        columns = first - FRONT + lax.broadcasted_iota(jnp.int32, (1, 2 * TILE), 1)
        source_allowed = columns <= source_ends
        target_allowed = first + lax.broadcasted_iota(jnp.int32, (1, TILE), 1) <= target_ends
        for head in range(2):
            raw = dot_nn(q_ref[head, pl.ds(first_row, TILE + ROWPAD), :], kt_ref[head, :, pl.ds(first, 2 * TILE)])
            raw = jnp.where(source_allowed, raw, 0.0)
            high = raw.astype(jnp.bfloat16)
            low = (raw - high.astype(jnp.float32)).astype(jnp.bfloat16)
            taps = dot_nn(high, thi_ref[head]) + dot_nn(low, thi_ref[head]) + dot_nn(high, tlo_ref[head])
            logits = taps[ROWPAD:, :TILE]
            for lag in range(1, lags):
                logits = logits + taps[ROWPAD - lag : ROWPAD - lag + TILE, lag * TILE : (lag + 1) * TILE]
            logits = jnp.where(target_allowed, logits, -1e30)
            c_ref[head, :, pl.ds(first, TILE)] = logits
            top_ref[head] = jnp.maximum(top_ref[head], logits)
        return carry

    lax.fori_loop(full, last + 1, mixed_step, 0)

    for head in range(2):
        top_ref[head] = jnp.broadcast_to(
            jnp.max(top_ref[head], axis=1, keepdims=True), (TILE, LANES)
        )

    def soft_tiles(first, width):
        for head in range(2):
            parts = []
            total = sum_ref[head]
            for part in range(width // LANES):
                logits = c_ref[head, :, pl.ds(first + part * LANES, LANES)]
                value = jnp.exp(logits - top_ref[head])
                total = total + value
                parts.append(value.astype(jnp.bfloat16))
            sum_ref[head] = total
            weights = parts[0] if len(parts) == 1 else jnp.concatenate(parts, axis=1)
            e_ref[head, :, pl.ds(first, width)] = weights
            o_ref[head] += dot_nn(weights, v_ref[0, pl.ds(first, width), :])

    def soft_step(pair, carry):
        soft_tiles(pl.multiple_of(pair * 2 * TILE, 2 * TILE), 2 * TILE)
        return carry

    lax.fori_loop(0, (last + 1) // 2, soft_step, 0)

    @pl.when(last % 2 == 0)
    def _():
        soft_tiles(pl.multiple_of(last * TILE, TILE), TILE)

    for head in range(2):
        inverse = 1.0 / jnp.sum(sum_ref[head], axis=1, keepdims=True)
        inv_ref[head] = jnp.broadcast_to(inverse, (TILE, LANES))
        o_ref[head] = o_ref[head] * inverse


def backward_kernel(
    bounds_ref, starts_ref, mix_ref, q_ref, kt_ref, k_ref, vt_ref, thi_ref, tlo_ref, ttr_ref,
    e_ref, o_ref, inv_ref, og_ref,
    dq_ref, dkt_ref, dvt_ref, gram_ref,
    kcat_ref, dkcat_ref, dqcat_ref, qcatt_ref, x_ref, xt_ref, delta_ref,
    *, lags, pics,
):
    group = pl.program_id(0)
    block = pl.program_id(1)
    blocks = pl.num_programs(1)
    first_row = pl.multiple_of(block * TILE, TILE)

    @pl.when(block == 0)
    def _():
        filter_keys(kt_ref, thi_ref, tlo_ref, kcat_ref, lags)
        dkcat_ref[...] = jnp.zeros(dkcat_ref.shape, jnp.float32)
        dq_ref[...] = jnp.zeros(dq_ref.shape, jnp.float32)
        dkt_ref[...] = jnp.zeros(dkt_ref.shape, jnp.float32)
        dvt_ref[...] = jnp.zeros(dvt_ref.shape, jnp.float32)
        gram_ref[...] = jnp.zeros(gram_ref.shape, jnp.float32)

    full = bounds_ref[block]
    last = bounds_ref[blocks + block]
    for head in range(2):
        rows = q_ref[head, pl.ds(first_row, TILE + ROWPAD), :].astype(jnp.float32)
        for lag in range(lags):
            turned = jnp.transpose(rows[ROWPAD - lag : ROWPAD - lag + TILE])
            qcatt_ref[head, lag * HD : (lag + 1) * HD, :] = turned[:HD].astype(jnp.bfloat16)
        dqcat_ref[head] = jnp.zeros(dqcat_ref.shape[1:], jnp.float32)
        inverse = inv_ref[head]
        delta = jnp.zeros((TILE, 1), jnp.float32)
        for out_head in range(2):
            weight = mix_ref[group * 4 + out_head * 2 + head]
            scaled = og_ref[out_head].astype(jnp.float32) * (inverse * weight)
            lanes = slice(out_head * LANES, (out_head + 1) * LANES)
            delta = delta + jnp.sum(scaled * o_ref[head, :, lanes], axis=1, keepdims=True)
            x_ref[head, :, lanes] = scaled.astype(jnp.bfloat16)
            xt_ref[head, lanes, :] = jnp.transpose(scaled).astype(jnp.bfloat16)
        delta_ref[head] = jnp.broadcast_to(delta, (TILE, LANES))

    def score_grads(head, first, width):
        prob_grads = dot_nn(x_ref[head], vt_ref[0, :, pl.ds(first, width)])
        weights = e_ref[head, :, pl.ds(first, width)]
        dvt_ref[0, :, pl.ds(first, width)] += dot_nn(xt_ref[head], weights)
        delta = delta_ref[head]
        parts = [
            weights[:, part * LANES : (part + 1) * LANES].astype(jnp.float32)
            * (prob_grads[:, part * LANES : (part + 1) * LANES] - delta)
            for part in range(width // LANES)
        ]
        return parts[0] if len(parts) == 1 else jnp.concatenate(parts, axis=1)

    def full_tiles(first, width):
        for head in range(2):
            grads = score_grads(head, first, width).astype(jnp.bfloat16)
            dqcat_ref[head] += dot_nt(grads, kcat_ref[head, :, pl.ds(first, width)])
            dkcat_ref[head, :, pl.ds(first, width)] += dot_nn(qcatt_ref[head], grads)

    def full_step(pair, carry):
        full_tiles(pl.multiple_of(pair * 2 * TILE, 2 * TILE), 2 * TILE)
        return carry

    lax.fori_loop(0, full // 2, full_step, 0)

    @pl.when(full % 2 == 1)
    def _():
        full_tiles(pl.multiple_of((full - 1) * TILE, TILE), TILE)

    source_rows = first_row - ROWPAD + lax.broadcasted_iota(jnp.int32, (TILE + ROWPAD, 1), 0)
    source_ends = row_ends(source_rows, starts_ref, pics)
    turned_rows = first_row - ROWPAD + lax.broadcasted_iota(jnp.int32, (1, TILE + ROWPAD), 1)
    turned_ends = row_ends(turned_rows, starts_ref, pics)

    def mixed_step(tile, carry):
        first = pl.multiple_of(tile * TILE, TILE)
        columns = first - FRONT + lax.broadcasted_iota(jnp.int32, (1, 2 * TILE), 1)
        turned_columns = first - FRONT + lax.broadcasted_iota(jnp.int32, (2 * TILE, 1), 0)
        for head in range(2):
            rows_low = q_ref[head, pl.ds(first_row, TILE + ROWPAD), :]
            grads = score_grads(head, first, TILE)
            padded = jnp.concatenate(
                [jnp.zeros((ROWPAD, TILE), jnp.float32), grads, jnp.zeros((8, TILE), jnp.float32)], axis=0
            )
            shifted = jnp.concatenate(
                [padded[lag : lag + TILE + ROWPAD] for lag in range(lags)], axis=1
            ).astype(jnp.bfloat16)
            raw_grads = jnp.where(columns <= source_ends, dot_nn(shifted, ttr_ref[head]), 0.0).astype(jnp.bfloat16)
            dq_ref[head, pl.ds(first_row, TILE + ROWPAD), :] += dot_nt(
                raw_grads, kt_ref[head, :, pl.ds(first, 2 * TILE)]
            )
            dkt_ref[head, :, pl.ds(first, 2 * TILE)] += dot_tn(rows_low, raw_grads)
            turned = dot_nt(k_ref[head, pl.ds(first, 2 * TILE), :], rows_low)
            turned = jnp.where(turned_columns <= turned_ends, turned, 0.0).astype(jnp.bfloat16)
            gram_ref[head] += dot_nn(turned, shifted)
        return carry

    lax.fori_loop(full, last + 1, mixed_step, 0)

    for head in range(2):
        parts = [dqcat_ref[head, :, lag * LANES : (lag + 1) * LANES] for lag in range(lags)]
        total = jnp.zeros((TILE + ROWPAD, LANES), jnp.float32)
        for lag in range(lags):
            pieces = [jnp.zeros((ROWPAD, LANES), jnp.float32), parts[lag], jnp.zeros((8, LANES), jnp.float32)]
            total = total + jnp.concatenate(pieces, axis=0)[lag : lag + TILE + ROWPAD]
        dq_ref[head, pl.ds(first_row, TILE + ROWPAD), :] += total

    @pl.when(block == blocks - 1)
    def _():
        for head in range(2):

            def tile_step(tile, carry):
                first = pl.multiple_of(tile * TILE, TILE)
                filtered = jnp.concatenate(
                    [dkcat_ref[head, lag * HD : (lag + 1) * HD, pl.ds(first, TILE)] for lag in range(lags)], axis=1
                ).astype(jnp.bfloat16)
                dkt_ref[head, :HD, pl.ds(first, 2 * TILE)] += dot_nn(filtered, ttr_ref[head])
                gram_ref[head] += dot_nn(k_ref[head, pl.ds(first, 2 * TILE), :HD], filtered)
                return carry

            lax.fori_loop(0, LEN // TILE, tile_step, 0)


def banded_taps(kernel, scale):
    heads, lags, taps = kernel.shape
    source = lax.broadcasted_iota(jnp.int32, (2 * TILE, TILE), 0)
    target = lax.broadcasted_iota(jnp.int32, (2 * TILE, TILE), 1)
    tap = target + FRONT + taps // 2 - source
    banded = jnp.zeros((heads, 2 * TILE, lags, TILE), jnp.float32)
    for index in range(taps):
        banded = jnp.where(
            (tap == index)[None, :, None, :], (kernel[:, :, index] * scale)[:, None, :, None], banded
        )
    return banded.reshape(heads, 2 * TILE, lags * TILE)


def gather_taps(gram, lags, taps, scale):
    heads = gram.shape[0]
    source = lax.broadcasted_iota(jnp.int32, (2 * TILE, TILE), 0)
    target = lax.broadcasted_iota(jnp.int32, (2 * TILE, TILE), 1)
    tap = target + FRONT + taps // 2 - source
    split = gram.reshape(heads, 2 * TILE, lags, TILE)
    sums = [
        jnp.sum(jnp.where((tap == index)[None, :, None, :], split, 0.0), axis=(1, 3)) for index in range(taps)
    ]
    return jnp.stack(sums, axis=2) * scale


def tile_bounds(starts):
    pics = starts.shape[0]
    blocks = LEN // TILE

    def ends(rows):
        found = rows
        for piece in range(pics):
            found = jnp.where(
                (rows >= starts[piece]) & (rows < starts[piece] + PIC), starts[piece] + PIC - 1, found
            )
        return found

    firsts = jnp.arange(blocks, dtype=jnp.int32) * TILE
    full = jnp.maximum((ends(firsts - 5) - 4) // TILE, 0)
    last = ends(firsts + TILE - 1) // TILE
    return jnp.concatenate([full, last])


def pad_heads(rows, heads, front, back):
    split = rows.reshape(LEN, heads, HD).transpose(1, 0, 2)
    return jnp.pad(split, ((0, 0), (front, back), (0, LANES - HD)))


def attention_inputs(queries, key_rows, values, kernel):
    heads = kernel.shape[0]
    q_pad = pad_heads(queries, heads, ROWPAD, 0)
    k_pad = pad_heads(key_rows, heads, FRONT, FRONT)
    kt_pad = k_pad.transpose(0, 2, 1)
    v_pad = pad_heads(values, heads, 0, 0)
    v_cat = v_pad.reshape(heads // 2, 2, LEN, LANES).transpose(0, 2, 1, 3).reshape(heads // 2, LEN, 2 * LANES)
    banded = banded_taps(kernel, 1.0 / math.sqrt(HD))
    thi = banded.astype(jnp.bfloat16)
    tlo = (banded - thi.astype(jnp.float32)).astype(jnp.bfloat16)
    return q_pad, k_pad, kt_pad, v_cat, thi, tlo


SMEM = pl.BlockSpec(memory_space=pltpu.SMEM)


def pair_spec(*shape):
    return pl.BlockSpec((2,) + shape, lambda group, block: (group,) + (0,) * len(shape))


def one_spec(*shape):
    return pl.BlockSpec((1,) + shape, lambda group, block: (group,) + (0,) * len(shape))


def row_spec(*shape):
    return pl.BlockSpec((2,) + shape, lambda group, block: (group, block) + (0,) * (len(shape) - 1))


def attention_forward(bounds, starts, q_pad, kt_pad, v_cat, thi, tlo, lags):
    heads = q_pad.shape[0]
    cols = LEN + 2 * FRONT
    return pl.pallas_call(
        functools.partial(forward_kernel, lags=lags, pics=starts.shape[0]),
        grid=(heads // 2, LEN // TILE),
        in_specs=[
            SMEM, SMEM,
            pair_spec(LEN + ROWPAD, LANES),
            pair_spec(LANES, cols),
            one_spec(LEN, 2 * LANES),
            pair_spec(2 * TILE, lags * TILE),
            pair_spec(2 * TILE, lags * TILE),
        ],
        out_specs=[row_spec(TILE, LEN), row_spec(TILE, 2 * LANES), row_spec(TILE, LANES)],
        out_shape=[
            jax.ShapeDtypeStruct((heads, LEN, LEN), jnp.bfloat16),
            jax.ShapeDtypeStruct((heads, LEN, 2 * LANES), jnp.float32),
            jax.ShapeDtypeStruct((heads, LEN, LANES), jnp.float32),
        ],
        scratch_shapes=[
            pltpu.VMEM((2, lags * LANES, LEN), jnp.bfloat16),
            pltpu.VMEM((2, TILE, LEN), jnp.float32),
            pltpu.VMEM((2, TILE, lags * LANES), jnp.bfloat16),
            pltpu.VMEM((2, TILE, LANES), jnp.float32),
            pltpu.VMEM((2, TILE, LANES), jnp.float32),
        ],
        compiler_params=pltpu.CompilerParams(vmem_limit_bytes=VMEM_BYTES),
        name="attention_forward",
    )(bounds, starts, q_pad, kt_pad, v_cat, thi, tlo)


def attention_backward(bounds, starts, mixing, q_pad, k_pad, kt_pad, v_cat, thi, tlo, e, o, inv, out_grads, lags):
    heads = q_pad.shape[0]
    cols = LEN + 2 * FRONT
    vt = v_cat.transpose(0, 2, 1)
    ttr = thi.transpose(0, 2, 1)
    return pl.pallas_call(
        functools.partial(backward_kernel, lags=lags, pics=starts.shape[0]),
        grid=(heads // 2, LEN // TILE),
        in_specs=[
            SMEM, SMEM, SMEM,
            pair_spec(LEN + ROWPAD, LANES),
            pair_spec(LANES, cols),
            pair_spec(cols, LANES),
            one_spec(2 * LANES, LEN),
            pair_spec(2 * TILE, lags * TILE),
            pair_spec(2 * TILE, lags * TILE),
            pair_spec(lags * TILE, 2 * TILE),
            row_spec(TILE, LEN), row_spec(TILE, 2 * LANES), row_spec(TILE, LANES),
            row_spec(TILE, LANES),
        ],
        out_specs=[
            pair_spec(LEN + ROWPAD, LANES),
            pair_spec(LANES, cols),
            one_spec(2 * LANES, LEN),
            pair_spec(2 * TILE, lags * TILE),
        ],
        out_shape=[
            jax.ShapeDtypeStruct((heads, LEN + ROWPAD, LANES), jnp.float32),
            jax.ShapeDtypeStruct((heads, LANES, cols), jnp.float32),
            jax.ShapeDtypeStruct((heads // 2, 2 * LANES, LEN), jnp.float32),
            jax.ShapeDtypeStruct((heads, 2 * TILE, lags * TILE), jnp.float32),
        ],
        scratch_shapes=[
            pltpu.VMEM((2, lags * LANES, LEN), jnp.bfloat16),
            pltpu.VMEM((2, lags * HD, LEN), jnp.float32),
            pltpu.VMEM((2, TILE, lags * LANES), jnp.float32),
            pltpu.VMEM((2, lags * HD, TILE), jnp.bfloat16),
            pltpu.VMEM((2, TILE, 2 * LANES), jnp.bfloat16),
            pltpu.VMEM((2, 2 * LANES, TILE), jnp.bfloat16),
            pltpu.VMEM((2, TILE, LANES), jnp.float32),
        ],
        compiler_params=pltpu.CompilerParams(vmem_limit_bytes=VMEM_BYTES),
        name="attention_backward",
    )(bounds, starts, mixing.reshape(-1), q_pad, kt_pad, k_pad, vt, thi, tlo, ttr, e, o, inv, out_grads)


def seq_forward(queries, key_rows, values, starts, kernel, mixing):
    heads, lags, taps = kernel.shape
    bounds = tile_bounds(starts)
    q_pad, k_pad, kt_pad, v_cat, thi, tlo = attention_inputs(queries, key_rows, values, kernel)
    e, o, inv = attention_forward(bounds, starts, q_pad, kt_pad, v_cat, thi, tlo, lags)
    split = o.reshape(heads // 2, 2, LEN, 2, LANES)[..., :HD]
    heads_out = jnp.einsum("gbiaf,gab->igaf", split, mixing, precision=lax.Precision.HIGHEST).reshape(LEN, heads, HD)
    return heads_out, (bounds, q_pad, k_pad, kt_pad, v_cat, thi, tlo, e, o, inv)


def seq_backward(saved, starts, kernel, mixing, out_grads):
    heads, lags, taps = kernel.shape
    bounds, q_pad, k_pad, kt_pad, v_cat, thi, tlo, e, o, inv = saved
    og = pad_heads(out_grads.reshape(LEN, heads * HD), heads, 0, 0)
    dq, dkt, dvt, gram = attention_backward(
        bounds, starts, mixing, q_pad, k_pad, kt_pad, v_cat, thi, tlo, e, o, inv, og, lags
    )
    query_back = dq[:, ROWPAD:, :HD].transpose(1, 0, 2).reshape(LEN, heads * HD).astype(jnp.bfloat16)
    key_back = dkt[:, :HD, FRONT : FRONT + LEN].transpose(2, 0, 1).reshape(LEN, heads * HD).astype(jnp.bfloat16)
    dv = dvt.reshape(heads // 2, 2, LANES, LEN)[:, :, :HD]
    value_back = dv.transpose(3, 0, 1, 2).reshape(LEN, heads * HD).astype(jnp.bfloat16)
    kernel_grad = gather_taps(gram, lags, taps, 1.0 / math.sqrt(HD))
    split = o.reshape(heads // 2, 2, LEN, 2, LANES)
    grads = og.reshape(heads // 2, 2, LEN, LANES).astype(jnp.float32)
    mixing_grad = jnp.sum(grads[:, :, None] * split.transpose(0, 3, 1, 2, 4), axis=(3, 4))
    return query_back, key_back, value_back, kernel_grad, mixing_grad


def rms_norm(values, gain):
    return values * lax.rsqrt(jnp.mean(values * values, axis=-1, keepdims=True) + epsilon) * gain


def group_norm(values, gain):
    centred = values - jnp.mean(values, axis=-1, keepdims=True)
    return centred * lax.rsqrt(jnp.mean(centred * centred, axis=-1, keepdims=True) + epsilon) * gain


def swiglu(gate, upper):
    return jax.nn.silu(gate) * upper


def project(left, right):
    return jnp.dot(left, right, preferred_element_type=jnp.float32)


def contract_rows(left, right):
    return lax.dot_general(
        left, right, (((0,), (0,)), ((), ())), preferred_element_type=jnp.float32
    )


def contract_cols(left, right):
    return lax.dot_general(
        left, right, (((1,), (1,)), ((), ())), preferred_element_type=jnp.float32
    )


def shards(
    layer_input,
    piece_starts,
    query_weight,
    key_weight,
    value_weight,
    out_weight,
    gate_weight,
    up_weight,
    down_weight,
    attention_gain,
    feedforward_gain,
    head_gain,
    score_kernel,
    head_mix,
    output_grad,
):
    width_local = query_weight.shape[1]
    heads_local = width_local // HD
    tensor_index = lax.axis_index("tensor")
    kernel_local = lax.dynamic_slice_in_dim(
        score_kernel, tensor_index * heads_local, heads_local, 0
    )
    mixing_local = lax.dynamic_slice_in_dim(
        head_mix, tensor_index * (heads_local // 2), heads_local // 2, 0
    )
    gain_local = lax.dynamic_slice_in_dim(head_gain, tensor_index * width_local, width_local, 0)
    local_rows = layer_input.shape[0]
    inputs = layer_input.astype(jnp.float32)
    normed, first_pull = jax.vjp(rms_norm, inputs, attention_gain)
    rows_all = lax.all_gather(normed.astype(jnp.bfloat16), "tensor", axis=0, tiled=True)
    query_full, key_full, value_full, out_full = (
        lax.all_gather(query_weight, "dp", axis=0, tiled=True),
        lax.all_gather(key_weight, "dp", axis=0, tiled=True),
        lax.all_gather(value_weight, "dp", axis=0, tiled=True),
        lax.all_gather(out_weight, "dp", axis=1, tiled=True),
    )
    queries = project(rows_all, query_full).astype(jnp.bfloat16)
    key_rows = project(rows_all, key_full).astype(jnp.bfloat16)
    values = project(rows_all, value_full).astype(jnp.bfloat16)
    starts = piece_starts[0]
    heads_out, saved = seq_forward(queries, key_rows, values, starts, kernel_local, mixing_local)
    normed_heads, group_pull = jax.vjp(group_norm, heads_out, gain_local.reshape(heads_local, HD))
    mixed_rows = normed_heads.astype(jnp.bfloat16).reshape(LEN, width_local)
    attended = lax.psum_scatter(
        project(
            lax.slice_in_dim(mixed_rows, 0, local_rows * lax.axis_size("tensor"), axis=0), out_full
        ).astype(jnp.bfloat16),
        "tensor",
        scatter_dimension=0,
        tiled=True,
    ).astype(jnp.float32)
    hidden = inputs + attended
    ffn_in, second_pull = jax.vjp(rms_norm, hidden, feedforward_gain)
    ffn_all = lax.all_gather(ffn_in.astype(jnp.bfloat16), "tensor", axis=0, tiled=True)
    gate_full, up_full, down_full = (
        lax.all_gather(gate_weight, "dp", axis=0, tiled=True),
        lax.all_gather(up_weight, "dp", axis=0, tiled=True),
        lax.all_gather(down_weight, "dp", axis=1, tiled=True),
    )
    gate = project(ffn_all, gate_full)
    upper = project(ffn_all, up_full)
    activated, act_pull = jax.vjp(swiglu, gate, upper)
    act_low = activated.astype(jnp.bfloat16)
    ffn_term = lax.psum_scatter(
        project(
            lax.slice_in_dim(act_low, 0, local_rows * lax.axis_size("tensor"), axis=0), down_full
        ).astype(jnp.bfloat16),
        "tensor",
        scatter_dimension=0,
        tiled=True,
    ).astype(jnp.float32)
    layer_output = (hidden + ffn_term).astype(jnp.bfloat16)
    query_back, key_back, value_back, out_back, gate_back, up_back, down_back = (
        lax.all_gather(query_weight, "dp", axis=0, tiled=True),
        lax.all_gather(key_weight, "dp", axis=0, tiled=True),
        lax.all_gather(value_weight, "dp", axis=0, tiled=True),
        lax.all_gather(out_weight, "dp", axis=1, tiled=True),
        lax.all_gather(gate_weight, "dp", axis=0, tiled=True),
        lax.all_gather(up_weight, "dp", axis=0, tiled=True),
        lax.all_gather(down_weight, "dp", axis=1, tiled=True),
    )
    grads_all = lax.all_gather(output_grad, "tensor", axis=0, tiled=True)
    act_grads = contract_cols(grads_all, down_back)
    down_part = contract_rows(act_low, grads_all)
    gate_grads, up_grads = act_pull(act_grads)
    gate_low = gate_grads.astype(jnp.bfloat16)
    up_low = up_grads.astype(jnp.bfloat16)
    gate_part = contract_rows(ffn_all, gate_low)
    up_part = contract_rows(ffn_all, up_low)
    gate_grad, up_grad, down_grad = (
        lax.psum_scatter(
            gate_part.astype(jnp.bfloat16), "dp", scatter_dimension=0, tiled=True
        ).astype(jnp.float32),
        lax.psum_scatter(
            up_part.astype(jnp.bfloat16), "dp", scatter_dimension=0, tiled=True
        ).astype(jnp.float32),
        lax.psum_scatter(
            down_part.astype(jnp.bfloat16), "dp", scatter_dimension=1, tiled=True
        ).astype(jnp.float32),
    )
    gate_rows = lax.slice_in_dim(gate_low, 0, local_rows * lax.axis_size("tensor"), axis=0)
    up_rows = lax.slice_in_dim(up_low, 0, local_rows * lax.axis_size("tensor"), axis=0)
    ffn_in_grad = lax.psum_scatter(
        (contract_cols(gate_rows, gate_back) + contract_cols(up_rows, up_back)).astype(
            jnp.bfloat16
        ),
        "tensor",
        scatter_dimension=0,
        tiled=True,
    ).astype(jnp.float32)
    hidden_part, feedforward_gain_part = second_pull(ffn_in_grad)
    hidden_grad = output_grad.astype(jnp.float32) + hidden_part
    attn_grads = lax.all_gather(hidden_grad.astype(jnp.bfloat16), "tensor", axis=0, tiled=True)
    mixed_grads = contract_cols(attn_grads, out_back)
    out_part = contract_rows(mixed_rows, attn_grads)
    head_grads, head_gain_part = group_pull(mixed_grads.reshape(LEN, heads_local, HD))
    head_low = head_grads.astype(jnp.bfloat16)
    query_low, key_low, value_low, kernel_part, mixing_part = seq_backward(
        saved, starts, kernel_local, mixing_local, head_low
    )
    query_part = contract_rows(rows_all, query_low)
    key_part = contract_rows(rows_all, key_low)
    value_part = contract_rows(rows_all, value_low)
    query_grad, key_grad, value_grad, out_weight_grad = (
        lax.psum_scatter(
            query_part.astype(jnp.bfloat16), "dp", scatter_dimension=0, tiled=True
        ).astype(jnp.float32),
        lax.psum_scatter(
            key_part.astype(jnp.bfloat16), "dp", scatter_dimension=0, tiled=True
        ).astype(jnp.float32),
        lax.psum_scatter(
            value_part.astype(jnp.bfloat16), "dp", scatter_dimension=0, tiled=True
        ).astype(jnp.float32),
        lax.psum_scatter(
            out_part.astype(jnp.bfloat16), "dp", scatter_dimension=1, tiled=True
        ).astype(jnp.float32),
    )
    total = contract_cols(query_low, query_back)
    total = total + contract_cols(key_low, key_back)
    normed_grad = lax.psum_scatter(
        (
            total
            + contract_cols(
                lax.slice_in_dim(value_low, 0, local_rows * lax.axis_size("tensor"), axis=0),
                value_back,
            )
        ).astype(jnp.bfloat16),
        "tensor",
        scatter_dimension=0,
        tiled=True,
    ).astype(jnp.float32)
    input_part, attention_gain_part = first_pull(normed_grad)
    input_grad = (hidden_grad + input_part).astype(jnp.bfloat16)
    head_gain_full = lax.dynamic_update_slice_in_dim(
        jnp.zeros(head_gain.shape, jnp.float32),
        head_gain_part.reshape(-1),
        tensor_index * width_local,
        0,
    )
    kernel_full = lax.dynamic_update_slice_in_dim(
        jnp.zeros(score_kernel.shape, jnp.float32),
        kernel_part,
        tensor_index * heads_local,
        0,
    )
    mixing_full = lax.dynamic_update_slice_in_dim(
        jnp.zeros(head_mix.shape, jnp.float32),
        mixing_part,
        tensor_index * (heads_local // 2),
        0,
    )
    attention_gain_grad, feedforward_gain_grad, head_gain_grad, score_kernel_grad, head_mix_grad = (
        lax.psum(
            (attention_gain_part, feedforward_gain_part, head_gain_full, kernel_full, mixing_full),
            ("dp", "tensor"),
        )
    )
    return (
        layer_output,
        input_grad,
        query_grad,
        key_grad,
        value_grad,
        out_weight_grad,
        gate_grad,
        up_grad,
        down_grad,
        attention_gain_grad,
        feedforward_gain_grad,
        head_gain_grad,
        score_kernel_grad,
        head_mix_grad,
    )


def solution(mesh):
    placed = (
        P(("dp", "tensor"), None),
        P("dp", None),
        P("dp", "tensor"),
        P("dp", "tensor"),
        P("dp", "tensor"),
        P("tensor", "dp"),
        P("dp", "tensor"),
        P("dp", "tensor"),
        P("tensor", "dp"),
        P(),
        P(),
        P(),
        P(),
        P(),
        P(("dp", "tensor"), None),
    )
    return jax.shard_map(
        shards,
        mesh=mesh,
        in_specs=placed,
        out_specs=(
            P(("dp", "tensor"), None),
            P(("dp", "tensor"), None),
            P("dp", "tensor"),
            P("dp", "tensor"),
            P("dp", "tensor"),
            P("tensor", "dp"),
            P("dp", "tensor"),
            P("dp", "tensor"),
            P("tensor", "dp"),
            P(),
            P(),
            P(),
            P(),
            P(),
        ),
        check_vma=False,
    )
```

```python
import functools
import math

import jax
import jax.numpy as jnp
from jax import lax
from jax.experimental import pallas as pl
from jax.experimental.pallas import tpu as pltpu
from jax.sharding import PartitionSpec as P

HD = 96
LEN = 1664
PIC = 256
TILE = 128
LANES = 128
FRONT = 64
ROWPAD = 16
COLS = LEN + 2 * FRONT
VMEM_BYTES = 56 * 1024 * 1024
epsilon = 1e-05


def dot_nn(left, right):
    return jnp.dot(left, right, preferred_element_type=jnp.float32)


def dot_nt(left, right):
    return lax.dot_general(left, right, (((1,), (1,)), ((), ())), preferred_element_type=jnp.float32)


def dot_tn(left, right):
    return lax.dot_general(left, right, (((0,), (0,)), ((), ())), preferred_element_type=jnp.float32)


def row_ends(rows, starts_ref, pics):
    ends = rows
    for piece in range(pics):
        first = starts_ref[piece]
        ends = jnp.where((rows >= first) & (rows < first + PIC), first + PIC - 1, ends)
    return ends


def stage_queries(qkv_ref, qpad_ref):
    for head in range(2):
        qpad_ref[head, :ROWPAD, :] = jnp.zeros((ROWPAD, LANES), jnp.bfloat16)
        qpad_ref[head, ROWPAD:, :] = qkv_ref[:, head * LANES : (head + 1) * LANES]


def stage_keys(qkv_ref, kpad_ref, kt_ref):
    for head in range(2):
        kpad_ref[head, :FRONT, :] = jnp.zeros((FRONT, LANES), jnp.bfloat16)
        kpad_ref[head, FRONT + LEN :, :] = jnp.zeros((FRONT, LANES), jnp.bfloat16)
        kpad_ref[head, FRONT : FRONT + LEN, :] = qkv_ref[:, (2 + head) * LANES : (3 + head) * LANES]

        def tile_step(tile, carry):
            first = pl.multiple_of(tile * TILE, TILE)
            rows = kpad_ref[head, pl.ds(first, TILE), :].astype(jnp.float32)
            kt_ref[head, :, pl.ds(first, TILE)] = jnp.transpose(rows).astype(jnp.bfloat16)
            return carry

        lax.fori_loop(0, COLS // TILE, tile_step, 0)


def filter_keys(kt_ref, thi_ref, tlo_ref, kcat_ref, lags):
    for head in range(2):

        def tile_step(tile, carry):
            first = pl.multiple_of(tile * TILE, TILE)
            window = kt_ref[head, :, pl.ds(first, 2 * TILE)]
            filtered = dot_nn(window, thi_ref[head]) + dot_nn(window, tlo_ref[head])
            for lag in range(lags):
                kcat_ref[head, lag * LANES : (lag + 1) * LANES, pl.ds(first, TILE)] = filtered[
                    :, lag * TILE : (lag + 1) * TILE
                ].astype(jnp.bfloat16)
            return carry

        lax.fori_loop(0, LEN // TILE, tile_step, 0)


def lagged(rows, lags):
    return jnp.concatenate(
        [rows[ROWPAD - lag : ROWPAD - lag + TILE] for lag in range(lags)], axis=1
    ).astype(jnp.bfloat16)


def centre(parts, weights):
    inside = lax.broadcasted_iota(jnp.int32, (TILE, LANES), 1) < HD
    mixed = parts[0] * weights[0] + parts[1] * weights[1]
    mean = jnp.sum(mixed, axis=1, keepdims=True) / HD
    centred = jnp.where(inside, mixed - mean, 0.0)
    spread = lax.rsqrt(jnp.sum(centred * centred, axis=1, keepdims=True) / HD + epsilon)
    return centred * spread, spread, inside


def forward_kernel(
    bounds_ref, starts_ref, mix_ref, gain_ref, qkv_ref, thi_ref, tlo_ref,
    e_ref, o_ref, inv_ref, z_ref,
    qpad_ref, kpad_ref, kt_ref, kcat_ref, c_ref, qcat_ref, top_ref, sum_ref,
    *, lags, pics, group,
):
    block = pl.program_id(0)
    blocks = pl.num_programs(0)
    first_row = pl.multiple_of(block * TILE, TILE)

    @pl.when(block == 0)
    def _():
        stage_queries(qkv_ref, qpad_ref)
        stage_keys(qkv_ref, kpad_ref, kt_ref)
        filter_keys(kt_ref, thi_ref, tlo_ref, kcat_ref, lags)

    full = bounds_ref[block]
    last = bounds_ref[blocks + block]
    for head in range(2):
        rows = qpad_ref[head, pl.ds(first_row, TILE + ROWPAD), :].astype(jnp.float32)
        qcat_ref[head] = lagged(rows, lags)
        top_ref[head] = jnp.full((TILE, LANES), -1e30, jnp.float32)
        sum_ref[head] = jnp.zeros((TILE, LANES), jnp.float32)
        o_ref[head] = jnp.zeros(o_ref.shape[1:], jnp.float32)

    def full_tiles(first, width):
        for head in range(2):
            logits = dot_nn(qcat_ref[head], kcat_ref[head, :, pl.ds(first, width)])
            c_ref[head, :, pl.ds(first, width)] = logits
            top = top_ref[head]
            for part in range(width // LANES):
                top = jnp.maximum(top, logits[:, part * LANES : (part + 1) * LANES])
            top_ref[head] = top

    def full_step(pair, carry):
        full_tiles(pl.multiple_of(pair * 2 * TILE, 2 * TILE), 2 * TILE)
        return carry

    lax.fori_loop(0, full // 2, full_step, 0)

    @pl.when(full % 2 == 1)
    def _():
        full_tiles(pl.multiple_of((full - 1) * TILE, TILE), TILE)

    source_rows = first_row - ROWPAD + lax.broadcasted_iota(jnp.int32, (TILE + ROWPAD, 1), 0)
    source_ends = row_ends(source_rows, starts_ref, pics)
    target_rows = first_row + lax.broadcasted_iota(jnp.int32, (TILE, 1), 0)
    target_ends = row_ends(target_rows, starts_ref, pics)

    def mixed_step(tile, carry):
        first = pl.multiple_of(tile * TILE, TILE)
        columns = first - FRONT + lax.broadcasted_iota(jnp.int32, (1, 2 * TILE), 1)
        source_allowed = columns <= source_ends
        target_allowed = first + lax.broadcasted_iota(jnp.int32, (1, TILE), 1) <= target_ends
        for head in range(2):
            raw = dot_nn(qpad_ref[head, pl.ds(first_row, TILE + ROWPAD), :], kt_ref[head, :, pl.ds(first, 2 * TILE)])
            raw = jnp.where(source_allowed, raw, 0.0)
            high = raw.astype(jnp.bfloat16)
            low = (raw - high.astype(jnp.float32)).astype(jnp.bfloat16)
            taps = dot_nn(high, thi_ref[head]) + dot_nn(low, thi_ref[head]) + dot_nn(high, tlo_ref[head])
            logits = taps[ROWPAD:, :TILE]
            for lag in range(1, lags):
                logits = logits + taps[ROWPAD - lag : ROWPAD - lag + TILE, lag * TILE : (lag + 1) * TILE]
            logits = jnp.where(target_allowed, logits, -1e30)
            c_ref[head, :, pl.ds(first, TILE)] = logits
            top_ref[head] = jnp.maximum(top_ref[head], logits)
        return carry

    lax.fori_loop(full, last + 1, mixed_step, 0)

    for head in range(2):
        top_ref[head] = jnp.broadcast_to(
            jnp.max(top_ref[head], axis=1, keepdims=True), (TILE, LANES)
        )

    def soft_tiles(first, width):
        for head in range(2):
            parts = []
            total = sum_ref[head]
            for part in range(width // LANES):
                logits = c_ref[head, :, pl.ds(first + part * LANES, LANES)]
                value = jnp.exp(logits - top_ref[head])
                total = total + value
                parts.append(value.astype(jnp.bfloat16))
            sum_ref[head] = total
            weights = parts[0] if len(parts) == 1 else jnp.concatenate(parts, axis=1)
            e_ref[head, :, pl.ds(first, width)] = weights
            o_ref[head] += dot_nn(weights, qkv_ref[pl.ds(first, width), 4 * LANES :])

    def soft_step(pair, carry):
        soft_tiles(pl.multiple_of(pair * 2 * TILE, 2 * TILE), 2 * TILE)
        return carry

    lax.fori_loop(0, (last + 1) // 2, soft_step, 0)

    @pl.when(last % 2 == 0)
    def _():
        soft_tiles(pl.multiple_of(last * TILE, TILE), TILE)

    for head in range(2):
        inverse = 1.0 / jnp.sum(sum_ref[head], axis=1, keepdims=True)
        inv_ref[head] = jnp.broadcast_to(inverse, (TILE, LANES))
        o_ref[head] = o_ref[head] * inverse
    for out_head in range(2):
        lanes = slice(out_head * LANES, (out_head + 1) * LANES)
        weights = [mix_ref[group * 4 + out_head * 2 + head] for head in range(2)]
        normal, _, _ = centre([o_ref[head, :, lanes] for head in range(2)], weights)
        z_ref[:, lanes] = (normal * gain_ref[:, lanes]).astype(jnp.bfloat16)


def fold_rows(values):
    return jnp.sum(values.reshape(TILE // 8, 8, LANES), axis=0)


def backward_kernel(
    bounds_ref, starts_ref, mix_ref, gain_ref, qkv_ref, thi_ref, tlo_ref, ttr_ref,
    e_ref, o_ref, inv_ref, dz_ref, *refs, lags, pics, group,
):
    (
        low_ref, gram_ref, dgain_ref, dmix_ref,
        qpad_ref, kpad_ref, kt_ref, vt_ref, kcat_ref,
        dq_ref, dkt_ref, dvt_ref, dkcat_ref, dqcat_ref, qcatt_ref, x_ref, xt_ref, delta_ref,
    ) = refs[-18:]
    block = pl.program_id(0)
    blocks = pl.num_programs(0)
    first_row = pl.multiple_of(block * TILE, TILE)

    @pl.when(block == 0)
    def _():
        stage_queries(qkv_ref, qpad_ref)
        stage_keys(qkv_ref, kpad_ref, kt_ref)
        filter_keys(kt_ref, thi_ref, tlo_ref, kcat_ref, lags)

        def tile_step(tile, carry):
            first = pl.multiple_of(tile * TILE, TILE)
            for head in range(2):
                rows = qkv_ref[pl.ds(first, TILE), (4 + head) * LANES : (5 + head) * LANES].astype(jnp.float32)
                vt_ref[head * LANES : (head + 1) * LANES, pl.ds(first, TILE)] = jnp.transpose(rows).astype(jnp.bfloat16)
            return carry

        lax.fori_loop(0, LEN // TILE, tile_step, 0)
        dkcat_ref[...] = jnp.zeros(dkcat_ref.shape, jnp.float32)
        dq_ref[...] = jnp.zeros(dq_ref.shape, jnp.float32)
        dkt_ref[...] = jnp.zeros(dkt_ref.shape, jnp.float32)
        dvt_ref[...] = jnp.zeros(dvt_ref.shape, jnp.float32)
        gram_ref[...] = jnp.zeros(gram_ref.shape, jnp.float32)
        dgain_ref[...] = jnp.zeros(dgain_ref.shape, jnp.float32)
        dmix_ref[...] = jnp.zeros(dmix_ref.shape, jnp.float32)

    full = bounds_ref[block]
    last = bounds_ref[blocks + block]
    out_grads = []
    for out_head in range(2):
        lanes = slice(out_head * LANES, (out_head + 1) * LANES)
        parts = [o_ref[head, :, lanes] for head in range(2)]
        weights = [mix_ref[group * 4 + out_head * 2 + head] for head in range(2)]
        normal, spread, inside = centre(parts, weights)
        grads = dz_ref[:, lanes].astype(jnp.float32)
        dgain_ref[0, :, lanes] += fold_rows(grads * normal)
        grads = grads * gain_ref[:, lanes]
        mean = jnp.sum(grads, axis=1, keepdims=True) / HD
        slope = jnp.sum(grads * normal, axis=1, keepdims=True) / HD
        grads = jnp.where(inside, (grads - mean - normal * slope) * spread, 0.0)
        grads = grads.astype(jnp.bfloat16).astype(jnp.float32)
        for head in range(2):
            dmix_ref[0, 2 * out_head + head] += fold_rows(grads * parts[head])
        out_grads.append(grads)
    for head in range(2):
        rows = qpad_ref[head, pl.ds(first_row, TILE + ROWPAD), :].astype(jnp.float32)
        for lag in range(lags):
            turned = jnp.transpose(rows[ROWPAD - lag : ROWPAD - lag + TILE])
            qcatt_ref[head, lag * HD : (lag + 1) * HD, :] = turned[:HD].astype(jnp.bfloat16)
        dqcat_ref[head] = jnp.zeros(dqcat_ref.shape[1:], jnp.float32)
        inverse = inv_ref[head]
        delta = jnp.zeros((TILE, 1), jnp.float32)
        for out_head in range(2):
            weight = mix_ref[group * 4 + out_head * 2 + head]
            scaled = out_grads[out_head] * (inverse * weight)
            lanes = slice(out_head * LANES, (out_head + 1) * LANES)
            delta = delta + jnp.sum(scaled * o_ref[head, :, lanes], axis=1, keepdims=True)
            x_ref[head, :, lanes] = scaled.astype(jnp.bfloat16)
            xt_ref[head, lanes, :] = jnp.transpose(scaled).astype(jnp.bfloat16)
        delta_ref[head] = jnp.broadcast_to(delta, (TILE, LANES))

    def score_grads(head, first, width):
        prob_grads = dot_nn(x_ref[head], vt_ref[:, pl.ds(first, width)])
        weights = e_ref[head, :, pl.ds(first, width)]
        dvt_ref[:, pl.ds(first, width)] += dot_nn(xt_ref[head], weights)
        delta = delta_ref[head]
        parts = [
            weights[:, part * LANES : (part + 1) * LANES].astype(jnp.float32)
            * (prob_grads[:, part * LANES : (part + 1) * LANES] - delta)
            for part in range(width // LANES)
        ]
        return parts[0] if len(parts) == 1 else jnp.concatenate(parts, axis=1)

    def full_tiles(first, width):
        for head in range(2):
            grads = score_grads(head, first, width).astype(jnp.bfloat16)
            dqcat_ref[head] += dot_nt(grads, kcat_ref[head, :, pl.ds(first, width)])
            dkcat_ref[head, :, pl.ds(first, width)] += dot_nn(qcatt_ref[head], grads)

    def full_step(pair, carry):
        full_tiles(pl.multiple_of(pair * 2 * TILE, 2 * TILE), 2 * TILE)
        return carry

    lax.fori_loop(0, full // 2, full_step, 0)

    @pl.when(full % 2 == 1)
    def _():
        full_tiles(pl.multiple_of((full - 1) * TILE, TILE), TILE)

    source_rows = first_row - ROWPAD + lax.broadcasted_iota(jnp.int32, (TILE + ROWPAD, 1), 0)
    source_ends = row_ends(source_rows, starts_ref, pics)
    turned_rows = first_row - ROWPAD + lax.broadcasted_iota(jnp.int32, (1, TILE + ROWPAD), 1)
    turned_ends = row_ends(turned_rows, starts_ref, pics)

    def mixed_step(tile, carry):
        first = pl.multiple_of(tile * TILE, TILE)
        columns = first - FRONT + lax.broadcasted_iota(jnp.int32, (1, 2 * TILE), 1)
        turned_columns = first - FRONT + lax.broadcasted_iota(jnp.int32, (2 * TILE, 1), 0)
        for head in range(2):
            rows_low = qpad_ref[head, pl.ds(first_row, TILE + ROWPAD), :]
            grads = score_grads(head, first, TILE)
            padded = jnp.concatenate(
                [jnp.zeros((ROWPAD, TILE), jnp.float32), grads, jnp.zeros((8, TILE), jnp.float32)], axis=0
            )
            shifted = jnp.concatenate(
                [padded[lag : lag + TILE + ROWPAD] for lag in range(lags)], axis=1
            ).astype(jnp.bfloat16)
            raw_grads = jnp.where(columns <= source_ends, dot_nn(shifted, ttr_ref[head]), 0.0).astype(jnp.bfloat16)
            dq_ref[head, pl.ds(first_row, TILE + ROWPAD), :] += dot_nt(
                raw_grads, kt_ref[head, :, pl.ds(first, 2 * TILE)]
            )
            dkt_ref[head, :, pl.ds(first, 2 * TILE)] += dot_tn(rows_low, raw_grads)
            turned = dot_nt(kpad_ref[head, pl.ds(first, 2 * TILE), :], rows_low)
            turned = jnp.where(turned_columns <= turned_ends, turned, 0.0).astype(jnp.bfloat16)
            gram_ref[head] += dot_nn(turned, shifted)
        return carry

    lax.fori_loop(full, last + 1, mixed_step, 0)

    for head in range(2):
        total = jnp.zeros((TILE + ROWPAD, LANES), jnp.float32)
        for lag in range(lags):
            part = dqcat_ref[head, :, lag * LANES : (lag + 1) * LANES]
            pieces = [jnp.zeros((ROWPAD, LANES), jnp.float32), part, jnp.zeros((8, LANES), jnp.float32)]
            total = total + jnp.concatenate(pieces, axis=0)[lag : lag + TILE + ROWPAD]
        dq_ref[head, pl.ds(first_row, TILE + ROWPAD), :] += total

    @pl.when(block == blocks - 1)
    def _():
        for head in range(2):

            def tile_step(tile, carry):
                first = pl.multiple_of(tile * TILE, TILE)
                filtered = jnp.concatenate(
                    [dkcat_ref[head, lag * HD : (lag + 1) * HD, pl.ds(first, TILE)] for lag in range(lags)], axis=1
                ).astype(jnp.bfloat16)
                dkt_ref[head, :HD, pl.ds(first, 2 * TILE)] += dot_nn(filtered, ttr_ref[head])
                gram_ref[head] += dot_nn(kpad_ref[head, pl.ds(first, 2 * TILE), :HD], filtered)
                return carry

            lax.fori_loop(0, LEN // TILE, tile_step, 0)
            low_ref[:, head * LANES : (head + 1) * LANES] = dq_ref[head, ROWPAD:, :].astype(jnp.bfloat16)

            def turn_step(tile, carry):
                first = pl.multiple_of(tile * TILE, TILE)
                half = TILE // 2
                lanes = slice((2 + head) * LANES, (3 + head) * LANES)
                front = jnp.transpose(dkt_ref[head, :, pl.ds(first, TILE)]).astype(jnp.bfloat16)
                back = jnp.transpose(dkt_ref[head, :, pl.ds(first + TILE, TILE)]).astype(jnp.bfloat16)
                low_ref[pl.ds(first, half), lanes] = front[half:]
                low_ref[pl.ds(first + half, half), lanes] = back[:half]
                lanes = slice((4 + head) * LANES, (5 + head) * LANES)
                turned = jnp.transpose(dvt_ref[head * LANES : (head + 1) * LANES, pl.ds(first, TILE)])
                low_ref[pl.ds(first, TILE), lanes] = turned.astype(jnp.bfloat16)
                return carry

            lax.fori_loop(0, LEN // TILE, turn_step, 0)


def banded_taps(kernel, scale):
    heads, lags, taps = kernel.shape
    source = lax.broadcasted_iota(jnp.int32, (2 * TILE, TILE), 0)
    target = lax.broadcasted_iota(jnp.int32, (2 * TILE, TILE), 1)
    tap = target + FRONT + taps // 2 - source
    banded = jnp.zeros((heads, 2 * TILE, lags, TILE), jnp.float32)
    for index in range(taps):
        banded = jnp.where(
            (tap == index)[None, :, None, :], (kernel[:, :, index] * scale)[:, None, :, None], banded
        )
    return banded.reshape(heads, 2 * TILE, lags * TILE)


def gather_taps(gram, lags, taps, scale):
    heads = gram.shape[0]
    source = lax.broadcasted_iota(jnp.int32, (2 * TILE, TILE), 0)
    target = lax.broadcasted_iota(jnp.int32, (2 * TILE, TILE), 1)
    tap = target + FRONT + taps // 2 - source
    split = gram.reshape(heads, 2 * TILE, lags, TILE)
    sums = [
        jnp.sum(jnp.where((tap == index)[None, :, None, :], split, 0.0), axis=(1, 3)) for index in range(taps)
    ]
    return jnp.stack(sums, axis=2) * scale


def tile_bounds(starts):
    blocks = LEN // TILE
    firsts = jnp.arange(blocks, dtype=jnp.int32) * TILE
    full = jnp.maximum((row_ends(firsts - 5, starts, starts.shape[0]) - 4) // TILE, 0)
    last = row_ends(firsts + TILE - 1, starts, starts.shape[0]) // TILE
    return jnp.concatenate([full, last])


SMEM = pl.BlockSpec(memory_space=pltpu.SMEM)


def pair_spec(group, *shape):
    return pl.BlockSpec((2,) + shape, lambda block: (group,) + (0,) * len(shape))


def row_spec(*shape):
    return pl.BlockSpec((2,) + shape, lambda block: (0, block) + (0,) * (len(shape) - 1))


def wide_spec(group, rows, width):
    return pl.BlockSpec((rows, width), lambda block: (0, group))


def tile_spec(width):
    return pl.BlockSpec((TILE, width), lambda block: (block, 0))


def attention_forward(group, bounds, starts, mixing, gain, qkv, thi, tlo, lags):
    return pl.pallas_call(
        functools.partial(forward_kernel, lags=lags, pics=starts.shape[0], group=group),
        grid=(LEN // TILE,),
        in_specs=[
            SMEM, SMEM, SMEM,
            wide_spec(group, 1, 2 * LANES),
            wide_spec(group, LEN, 6 * LANES),
            pair_spec(group, 2 * TILE, lags * TILE),
            pair_spec(group, 2 * TILE, lags * TILE),
        ],
        out_specs=[
            row_spec(TILE, LEN), row_spec(TILE, 2 * LANES), row_spec(TILE, LANES),
            tile_spec(2 * LANES),
        ],
        out_shape=[
            jax.ShapeDtypeStruct((2, LEN, LEN), jnp.bfloat16),
            jax.ShapeDtypeStruct((2, LEN, 2 * LANES), jnp.float32),
            jax.ShapeDtypeStruct((2, LEN, LANES), jnp.float32),
            jax.ShapeDtypeStruct((LEN, 2 * LANES), jnp.bfloat16),
        ],
        scratch_shapes=[
            pltpu.VMEM((2, LEN + ROWPAD, LANES), jnp.bfloat16),
            pltpu.VMEM((2, COLS, LANES), jnp.bfloat16),
            pltpu.VMEM((2, LANES, COLS), jnp.bfloat16),
            pltpu.VMEM((2, lags * LANES, LEN), jnp.bfloat16),
            pltpu.VMEM((2, TILE, LEN), jnp.float32),
            pltpu.VMEM((2, TILE, lags * LANES), jnp.bfloat16),
            pltpu.VMEM((2, TILE, LANES), jnp.float32),
            pltpu.VMEM((2, TILE, LANES), jnp.float32),
        ],
        compiler_params=pltpu.CompilerParams(vmem_limit_bytes=VMEM_BYTES),
        cost_estimate=pl.CostEstimate(flops=70_000_000_000, transcendentals=0, bytes_accessed=20_000_000),
        name="attention_forward",
    )(bounds, starts, mixing.reshape(-1), gain, qkv, thi, tlo)


def attention_backward(group, bounds, starts, mixing, gain, qkv, thi, tlo, ttr, e, o, inv, dz, low, lags):
    width = qkv.shape[1]
    joined = [] if low is None else [low]
    return pl.pallas_call(
        functools.partial(backward_kernel, lags=lags, pics=starts.shape[0], group=group),
        grid=(LEN // TILE,),
        in_specs=[
            SMEM, SMEM, SMEM,
            wide_spec(group, 1, 2 * LANES),
            wide_spec(group, LEN, 6 * LANES),
            pair_spec(group, 2 * TILE, lags * TILE),
            pair_spec(group, 2 * TILE, lags * TILE),
            pair_spec(group, lags * TILE, 2 * TILE),
            row_spec(TILE, LEN), row_spec(TILE, 2 * LANES), row_spec(TILE, LANES),
            tile_spec(2 * LANES),
        ] + [pl.BlockSpec(memory_space=pl.ANY)] * len(joined),
        out_specs=[
            wide_spec(group, LEN, 6 * LANES),
            pair_spec(0, 2 * TILE, lags * TILE),
            pl.BlockSpec((1, 8, 2 * LANES), lambda block: (0, 0, 0)),
            pl.BlockSpec((1, 4, 8, LANES), lambda block: (0, 0, 0, 0)),
        ],
        out_shape=[
            jax.ShapeDtypeStruct((LEN, width), jnp.bfloat16),
            jax.ShapeDtypeStruct((2, 2 * TILE, lags * TILE), jnp.float32),
            jax.ShapeDtypeStruct((1, 8, 2 * LANES), jnp.float32),
            jax.ShapeDtypeStruct((1, 4, 8, LANES), jnp.float32),
        ],
        scratch_shapes=[
            pltpu.VMEM((2, LEN + ROWPAD, LANES), jnp.bfloat16),
            pltpu.VMEM((2, COLS, LANES), jnp.bfloat16),
            pltpu.VMEM((2, LANES, COLS), jnp.bfloat16),
            pltpu.VMEM((2 * LANES, LEN), jnp.bfloat16),
            pltpu.VMEM((2, lags * LANES, LEN), jnp.bfloat16),
            pltpu.VMEM((2, LEN + ROWPAD, LANES), jnp.float32),
            pltpu.VMEM((2, LANES, COLS), jnp.float32),
            pltpu.VMEM((2 * LANES, LEN), jnp.float32),
            pltpu.VMEM((2, lags * HD, LEN), jnp.float32),
            pltpu.VMEM((2, TILE, lags * LANES), jnp.float32),
            pltpu.VMEM((2, lags * HD, TILE), jnp.bfloat16),
            pltpu.VMEM((2, TILE, 2 * LANES), jnp.bfloat16),
            pltpu.VMEM((2, 2 * LANES, TILE), jnp.bfloat16),
            pltpu.VMEM((2, TILE, LANES), jnp.float32),
        ],
        compiler_params=pltpu.CompilerParams(vmem_limit_bytes=VMEM_BYTES),
        cost_estimate=pl.CostEstimate(flops=115_000_000_000, transcendentals=0, bytes_accessed=20_000_000),
        input_output_aliases={12: 0} if joined else {},
        name="attention_backward",
    )(bounds, starts, mixing.reshape(-1), gain, qkv, thi, tlo, ttr, e, o, inv, dz, *joined)


def pad_heads(columns, heads):
    rows = columns.shape[0]
    split = columns.reshape(rows, heads, HD)
    return jnp.pad(split, ((0, 0), (0, 0), (0, LANES - HD)))


def drop_pads(columns, heads):
    rows = columns.shape[0]
    return columns.reshape(rows, heads, LANES)[:, :, :HD].reshape(rows, heads * HD)


def join_pairs(queries, key_rows, values, heads):
    rows = queries.shape[0]
    parts = [pad_heads(part, heads).reshape(rows, heads // 2, 2, LANES) for part in (queries, key_rows, values)]
    return jnp.stack(parts, axis=2).reshape(rows, heads * 3 * LANES)


def split_pairs(columns, heads):
    rows = columns.shape[0]
    split = columns.reshape(rows, heads // 2, 3, 2, LANES)[..., :HD]
    return [split[:, :, part].reshape(rows, heads * HD) for part in range(3)]


def rms_norm(values, gain):
    return values * lax.rsqrt(jnp.mean(values * values, axis=-1, keepdims=True) + epsilon) * gain


def swiglu(gate, upper):
    return jax.nn.silu(gate) * upper


def shift(values, step):
    size = lax.axis_size("tensor")
    return lax.ppermute(values, "tensor", [(index, (index + step) % size) for index in range(size)])


def swap(values):
    size = lax.axis_size("tensor")
    return lax.ppermute(values, "tensor", [(index, index ^ 1) for index in range(size)])


def line_gather(rows, chunks):
    size = lax.axis_size("tensor")
    index = lax.axis_index("tensor")
    count = rows.shape[0]
    part = count // chunks
    gathered = jnp.zeros((size * count,) + rows.shape[1:], rows.dtype)
    gathered = lax.dynamic_update_slice_in_dim(gathered, rows, index * count, 0)
    rising = [rows[chunk * part : (chunk + 1) * part] for chunk in range(chunks)]
    falling = list(rising)
    from_below, from_above = [], []
    for step in range(1, size):
        upward = [(i, i + 1) for i in range(size - 1) if i >= step - 1]
        downward = [(i + 1, i) for i in range(size - 1) if i + 1 <= size - step]
        for chunk in range(chunks):
            rising[chunk] = lax.ppermute(rising[chunk], "tensor", upward)
            falling[chunk] = lax.ppermute(falling[chunk], "tensor", downward)
        from_below.append(list(rising))
        from_above.append(list(falling))
    for step in range(1, size):
        first = ((index - step) % size) * count
        for chunk in range(chunks):
            piece = jnp.where(index >= step, from_below[step - 1][chunk], from_above[size - step - 1][chunk])
            gathered = lax.dynamic_update_slice_in_dim(gathered, piece, first + chunk * part, 0)
    return gathered


def line_scatter(parts, count):
    size = lax.axis_size("tensor")
    index = lax.axis_index("tensor")

    def block(values, position):
        first = jnp.clip(position, 0, size - 1) * count
        return lax.dynamic_slice_in_dim(values, first, count, 0).astype(jnp.float32)

    rising = [None] * len(parts)
    falling = [None] * len(parts)
    for step in range(1, size):
        upward = [(i, i + 1) for i in range(size - 1) if i <= step - 1]
        downward = [(i + 1, i) for i in range(size - 1) if size - 2 - i <= step - 1]
        for chunk, values in enumerate(parts):
            up = block(values, size - step + index)
            down = block(values, step + index - size)
            if step > 1:
                up = up + rising[chunk].astype(jnp.float32)
                down = down + falling[chunk].astype(jnp.float32)
            rising[chunk] = lax.ppermute(up.astype(jnp.bfloat16), "tensor", upward)
            falling[chunk] = lax.ppermute(down.astype(jnp.bfloat16), "tensor", downward)
    sums = [
        block(values, index) + (rising[chunk].astype(jnp.float32) + falling[chunk].astype(jnp.float32))
        for chunk, values in enumerate(parts)
    ]
    return jnp.concatenate(sums, axis=1)


def sum_all(values):
    for axis in ("tensor", "dp"):
        size = lax.axis_size(axis)
        step = 1
        while step < size:
            values = values + lax.ppermute(values, axis, [(i, i ^ step) for i in range(size)])
            step *= 2
    return values


def after(values, *others):
    return lax.optimization_barrier((values,) + others)[0]


def shards(
    layer_input,
    piece_starts,
    query_weight,
    key_weight,
    value_weight,
    out_weight,
    gate_weight,
    up_weight,
    down_weight,
    attention_gain,
    feedforward_gain,
    head_gain,
    score_kernel,
    head_mix,
    output_grad,
):
    size = lax.axis_size("tensor")
    index = lax.axis_index("tensor")
    width_local = query_weight.shape[1]
    heads = width_local // HD
    pairs = heads // 2
    wide = 2 * LANES
    hidden_local = gate_weight.shape[1]
    count = layer_input.shape[0]
    lags, taps = score_kernel.shape[1:]
    score_scale = 1.0 / math.sqrt(HD)

    inputs = layer_input.astype(jnp.float32)
    normed, first_pull = jax.vjp(rms_norm, inputs, attention_gain)
    normed_low = normed.astype(jnp.bfloat16)
    rows_all = line_gather(normed_low, 2)

    query_weight, key_weight, value_weight = after((query_weight, key_weight, value_weight), normed_low)
    qkv_full = lax.all_gather(
        join_pairs(query_weight, key_weight, value_weight, heads), "dp", axis=0, tiled=True
    )
    kernel_local = lax.dynamic_slice_in_dim(score_kernel, index * heads, heads, 0)
    mixing_local = lax.dynamic_slice_in_dim(head_mix, index * pairs, pairs, 0)
    gain_local = lax.dynamic_slice_in_dim(head_gain, index * width_local, width_local, 0)
    gain_pad = pad_heads(gain_local[None], heads).reshape(1, heads * LANES)
    starts = piece_starts[0]
    bounds = tile_bounds(starts)
    banded = banded_taps(kernel_local, score_scale)
    taps_high = banded.astype(jnp.bfloat16)
    taps_low = (banded - taps_high.astype(jnp.float32)).astype(jnp.bfloat16)
    taps_turned = taps_high.transpose(0, 2, 1)

    out_own = pad_heads(after(out_weight, rows_all).T, heads).reshape(-1, heads * LANES)
    out_parts = [out_own] + [shift(out_own, step) for step in range(1, size)]
    out_full = lax.all_gather(
        jnp.concatenate(
            [part[:, pair * wide : (pair + 1) * wide] for pair in range(pairs) for part in out_parts], axis=1
        ),
        "dp", axis=0, tiled=True,
    )
    qkv = dot_nn(rows_all, qkv_full).astype(jnp.bfloat16)
    qkv, taps_high, taps_low, taps_turned = lax.optimization_barrier((qkv, taps_high, taps_low, taps_turned))
    gate_up_own = after(jnp.concatenate([gate_weight, up_weight], axis=1), rows_all)
    down_own = after(down_weight.T, rows_all)
    gate_up = [gate_up_own] + [shift(gate_up_own, step) for step in range(2, size, 2)]
    down = [down_own] + [shift(down_own, step) for step in range(2, size, 2)]
    grads_swapped = swap(after(output_grad, rows_all))

    saved = []
    token_parts = []
    for pair in range(pairs):
        weights, parts_out, inverse, normed_heads = attention_forward(
            pair, bounds, starts, mixing_local, gain_pad, qkv, taps_high, taps_low, lags
        )
        saved.append((weights, parts_out, inverse))
        if pair == 0:
            gate_up, down, grads_swapped = after((gate_up, down, grads_swapped), normed_heads)
        for step in range(size):
            first = ((index + step) % size) * count
            part = lax.dynamic_slice_in_dim(normed_heads, first, count, 0)
            token_parts.append(part if step == 0 else shift(part, step))
    token_heads = jnp.concatenate(token_parts, axis=1)
    grads_two = jnp.concatenate([output_grad, grads_swapped], axis=0)

    gate_up_full = lax.all_gather(
        jnp.concatenate([part[:, :hidden_local] for part in gate_up] + [part[:, hidden_local:] for part in gate_up], axis=1),
        "dp", axis=0, tiled=True,
    )
    down_full = lax.all_gather(jnp.concatenate(down, axis=1), "dp", axis=0, tiled=True)
    hidden_width = down_full.shape[1]
    gate_full = gate_up_full[:, :hidden_width]
    up_full = gate_up_full[:, hidden_width:]

    hidden = inputs + dot_nt(token_heads, out_full)
    ffn_in, second_pull = jax.vjp(rms_norm, hidden, feedforward_gain)
    ffn_low = ffn_in.astype(jnp.bfloat16)
    ffn_two = jnp.concatenate([ffn_low, swap(ffn_low)], axis=0)
    gate = dot_nn(ffn_two, gate_full)
    upper = dot_nn(ffn_two, up_full)
    activated, act_pull = jax.vjp(swiglu, gate, upper)
    act_low = activated.astype(jnp.bfloat16)
    down_part = dot_tn(grads_two, act_low).astype(jnp.bfloat16)
    down_sum = lax.psum_scatter(down_part, "dp", scatter_dimension=0, tiled=True)
    act_grads = dot_nn(after(grads_two, down_part), down_full)
    gate_grads, up_grads = act_pull(act_grads)
    gate_low = gate_grads.astype(jnp.bfloat16)
    up_low = up_grads.astype(jnp.bfloat16)

    def ffn_back(rows):
        return dot_nt(gate_low[rows], gate_full) + dot_nt(up_low[rows], up_full)

    ffn_back_sent = ffn_back(slice(count, None)).astype(jnp.bfloat16)
    ffn_back_kept = ffn_back(slice(0, count))
    ffn_two_later, gate_later, up_later = after((ffn_two, gate_low, up_low), ffn_back_kept, ffn_back_sent)
    gate_up_part = dot_tn(ffn_two_later, jnp.concatenate([gate_later, up_later], axis=1)).astype(jnp.bfloat16)
    gate_up_sum = lax.psum_scatter(gate_up_part, "dp", scatter_dimension=0, tiled=True)
    ffn_in_grad = ffn_back_kept + after(swap(ffn_back_sent), gate_up_part).astype(jnp.float32)
    hidden_part, feedforward_gain_part = second_pull(ffn_in_grad)
    hidden_grad = output_grad.astype(jnp.float32) + hidden_part
    hidden_low = hidden_grad.astype(jnp.bfloat16)

    head_back = dot_nn(hidden_low, out_full).astype(jnp.bfloat16)
    head_grads = []
    for pair in range(pairs):
        rows = jnp.zeros((LEN, wide), jnp.bfloat16)
        for step in range(size):
            first = (pair * size + step) * wide
            part = head_back[:, first : first + wide]
            part = part if step == 0 else shift(part, -step)
            rows = lax.dynamic_update_slice_in_dim(rows, part, ((index + step) % size) * count, 0)
        head_grads.append(rows)

    act_later, hidden_later = after((act_low, hidden_low), head_back)
    out_part = dot_tn(hidden_later, token_heads).astype(jnp.bfloat16)
    ffn_out_sent = dot_nt(act_later[count:], down_full).astype(jnp.bfloat16)
    ffn_term = dot_nt(act_later[:count], down_full) + swap(ffn_out_sent).astype(jnp.float32)
    layer_output = (hidden + ffn_term).astype(jnp.bfloat16)

    head_grads[0] = after(head_grads[0], out_part, ffn_out_sent)
    def owned(groups, stride):
        joined = jnp.concatenate(groups[0], axis=1).astype(jnp.float32)
        for step in range(1, len(groups)):
            joined = joined + shift(jnp.concatenate(groups[step], axis=1), -step * stride).astype(jnp.float32)
        return joined

    def columns(values, first, width):
        return values[:, first * width : (first + 1) * width]

    low = None
    grams, gain_parts, mixing_parts = [], [], []
    for pair in range(pairs):
        if pair == pairs - 1:
            head_grads[pair], gate_up_sum, down_sum = lax.optimization_barrier(
                (head_grads[pair], gate_up_sum, down_sum)
            )
        low, gram, gain_part, mixing_part = attention_backward(
            pair, bounds, starts, mixing_local, gain_pad, qkv, taps_high, taps_low, taps_turned,
            *saved[pair], head_grads[pair], low, lags,
        )
        if pair == 0:
            out_sum = lax.psum_scatter(after(out_part, gram), "dp", scatter_dimension=0, tiled=True)
        grams.append(gram)
        gain_parts.append(gain_part)
        mixing_parts.append(mixing_part)
    gram = jnp.concatenate(grams, axis=0)
    gain_parts = jnp.concatenate(gain_parts, axis=0)
    mixing_parts = jnp.concatenate(mixing_parts, axis=0)
    parts = hidden_width // hidden_local
    ffn_sum = owned(
        [
            [columns(gate_up_sum, part, hidden_local), columns(gate_up_sum, parts + part, hidden_local),
             columns(down_sum, part, hidden_local)]
            for part in range(parts)
        ],
        2,
    )
    low, ffn_sum, out_sum = lax.optimization_barrier((low, ffn_sum, out_sum))
    gate_grad, up_grad, down_grad = [columns(ffn_sum, part, hidden_local) for part in range(3)]
    down_grad = down_grad.T

    half = qkv_full.shape[0] // 2
    normed_parts = [
        dot_nt(low, qkv_full[chunk * half : (chunk + 1) * half]).astype(jnp.bfloat16) for chunk in range(2)
    ]
    attention_gain_part = jnp.concatenate(
        [
            jnp.sum(
                part.astype(jnp.float32) * rows_all[:, chunk * half : (chunk + 1) * half].astype(jnp.float32), axis=0
            )
            for chunk, part in enumerate(normed_parts)
        ]
    ) / attention_gain
    normed_grad = line_scatter(normed_parts, count)
    qkv_part = dot_tn(after(rows_all, *normed_parts), low).astype(jnp.bfloat16)
    qkv_sum = lax.psum_scatter(qkv_part, "dp", scatter_dimension=0, tiled=True).astype(jnp.float32)
    input_part = first_pull(normed_grad)[0]
    input_grad = (hidden_grad + input_part).astype(jnp.bfloat16)
    query_grad, key_grad, value_grad = split_pairs(qkv_sum, heads)
    out_total = owned(
        [[columns(out_sum, pair * size + step, wide) for pair in range(pairs)] for step in range(size)], 1
    )
    out_weight_grad = drop_pads(out_total, heads).T

    kernel_part = gather_taps(gram, lags, taps, score_scale)
    mixing_part = jnp.sum(mixing_parts, axis=(2, 3)).reshape(mixing_local.shape)
    head_gain_part = drop_pads(jnp.sum(gain_parts, axis=1).reshape(1, heads * LANES), heads).reshape(-1)

    def placed(part, whole, first):
        return lax.dynamic_update_slice_in_dim(jnp.zeros(whole.shape, jnp.float32), part, first, 0)

    small = (
        attention_gain_part,
        feedforward_gain_part,
        placed(head_gain_part, head_gain, index * width_local),
        placed(kernel_part, score_kernel, index * heads),
        placed(mixing_part, head_mix, index * pairs),
    )
    packed = jnp.concatenate([part.reshape(-1) for part in small])
    packed = jnp.pad(packed, (0, -packed.shape[0] % 1024)).reshape(-1, LANES)
    packed = sum_all(packed).reshape(-1)
    sums = []
    first = 0
    for part in small:
        sums.append(packed[first : first + part.size].reshape(part.shape))
        first += part.size
    return (
        layer_output,
        input_grad,
        query_grad,
        key_grad,
        value_grad,
        out_weight_grad,
        gate_grad,
        up_grad,
        down_grad,
        *sums,
    )


def solution(mesh):
    placed = (
        P(("dp", "tensor"), None),
        P("dp", None),
        P("dp", "tensor"),
        P("dp", "tensor"),
        P("dp", "tensor"),
        P("tensor", "dp"),
        P("dp", "tensor"),
        P("dp", "tensor"),
        P("tensor", "dp"),
        P(),
        P(),
        P(),
        P(),
        P(),
        P(("dp", "tensor"), None),
    )
    return jax.shard_map(
        shards,
        mesh=mesh,
        in_specs=placed,
        out_specs=(
            P(("dp", "tensor"), None),
            P(("dp", "tensor"), None),
            P("dp", "tensor"),
            P("dp", "tensor"),
            P("dp", "tensor"),
            P("tensor", "dp"),
            P("dp", "tensor"),
            P("dp", "tensor"),
            P("tensor", "dp"),
            P(),
            P(),
            P(),
            P(),
            P(),
        ),
        check_vma=False,
    )
```

```python
import functools
import math

import jax
import jax.numpy as jnp
from jax import lax
from jax.experimental import pallas as pl
from jax.experimental.pallas import tpu as pltpu
from jax.sharding import PartitionSpec as P

HD = 96
LEN = 1664
PIC = 256
TILE = 128
LANES = 128
FRONT = 64
ROWPAD = 16
COLS = LEN + 2 * FRONT
GROUP = 8
VMEM_BYTES = 56 * 1024 * 1024
epsilon = 1e-05


def dot_nn(left, right):
    return jnp.dot(left, right, preferred_element_type=jnp.float32)


def dot_nt(left, right):
    return lax.dot_general(left, right, (((1,), (1,)), ((), ())), preferred_element_type=jnp.float32)


def dot_tn(left, right):
    return lax.dot_general(left, right, (((0,), (0,)), ((), ())), preferred_element_type=jnp.float32)


def row_ends(rows, starts_ref, pics):
    ends = rows
    for piece in range(pics):
        first = starts_ref[piece]
        ends = jnp.where((rows >= first) & (rows < first + PIC), first + PIC - 1, ends)
    return ends


def over_tiles(tiles, work):
    def wide_step(group, carry):
        work(pl.multiple_of(group * GROUP * TILE, GROUP * TILE), GROUP * TILE)
        return carry

    lax.fori_loop(0, tiles // GROUP, wide_step, 0)
    left = tiles % GROUP
    size = GROUP // 2
    while size:
        first = tiles - left % (2 * size)

        @pl.when((left // size) % 2 == 1)
        def _():
            work(pl.multiple_of(first * TILE, TILE), size * TILE)

        size //= 2


def over_edges(first, end, work):
    def pair_step(pair, carry):
        work(pl.multiple_of((first + 2 * pair) * TILE, TILE), 2 * TILE)
        return carry

    lax.fori_loop(0, (end - first) // 2, pair_step, 0)

    @pl.when((end - first) % 2 == 1)
    def _():
        work(pl.multiple_of((end - 1) * TILE, TILE), TILE)


def stage_queries(qkv_ref, qpad_ref):
    for head in range(2):
        qpad_ref[head, :ROWPAD, :] = jnp.zeros((ROWPAD, LANES), jnp.bfloat16)
        qpad_ref[head, ROWPAD:, :] = qkv_ref[:, head * LANES : (head + 1) * LANES]


def stage_keys(qkv_ref, kpad_ref, kt_ref):
    for head in range(2):
        kpad_ref[head, :FRONT, :] = jnp.zeros((FRONT, LANES), jnp.bfloat16)
        kpad_ref[head, FRONT + LEN :, :] = jnp.zeros((FRONT, LANES), jnp.bfloat16)
        kpad_ref[head, FRONT : FRONT + LEN, :] = qkv_ref[:, (2 + head) * LANES : (3 + head) * LANES]

        def tile_step(tile, carry):
            first = pl.multiple_of(tile * TILE, TILE)
            rows = kpad_ref[head, pl.ds(first, TILE), :].astype(jnp.float32)
            kt_ref[head, :, pl.ds(first, TILE)] = jnp.transpose(rows).astype(jnp.bfloat16)
            return carry

        lax.fori_loop(0, COLS // TILE, tile_step, 0)


def filter_keys(kt_ref, thi_ref, tlo_ref, stack_ref, kcat_ref, lags):
    tiles = LEN // TILE
    for head in range(2):
        for tile in range(tiles):
            stack_ref[tile * TILE : (tile + 1) * TILE, :] = kt_ref[head, :, tile * TILE : (tile + 2) * TILE]
        for first in range(0, lags, 2):
            width = min(2, lags - first) * TILE
            lanes = slice(first * TILE, first * TILE + width)
            filtered = dot_nn(stack_ref[...], thi_ref[head, :, lanes]) + dot_nn(stack_ref[...], tlo_ref[head, :, lanes])
            for tile in range(tiles):
                for part in range(width // TILE):
                    lag = first + part
                    kcat_ref[head, lag * LANES : (lag + 1) * LANES, tile * TILE : (tile + 1) * TILE] = filtered[
                        tile * TILE : (tile + 1) * TILE, part * TILE : (part + 1) * TILE
                    ].astype(jnp.bfloat16)


def lagged(rows, lags):
    return jnp.concatenate(
        [rows[ROWPAD - lag : ROWPAD - lag + TILE] for lag in range(lags)], axis=1
    ).astype(jnp.bfloat16)


def centre(parts, weights):
    inside = lax.broadcasted_iota(jnp.int32, (TILE, LANES), 1) < HD
    mixed = parts[0] * weights[0] + parts[1] * weights[1]
    mean = jnp.sum(mixed, axis=1, keepdims=True) / HD
    centred = jnp.where(inside, mixed - mean, 0.0)
    spread = lax.rsqrt(jnp.sum(centred * centred, axis=1, keepdims=True) / HD + epsilon)
    return centred * spread, spread, inside


def forward_kernel(
    bounds_ref, starts_ref, mix_ref, gain_ref, qkv_ref, thi_ref, tlo_ref,
    e_ref, o_ref, inv_ref, z_ref,
    qpad_ref, kpad_ref, kt_ref, stack_ref, kcat_ref, c_ref, qcat_ref, top_ref, sum_ref,
    *, lags, pics, group,
):
    block = pl.program_id(0)
    blocks = pl.num_programs(0)
    first_row = pl.multiple_of(block * TILE, TILE)

    @pl.when(block == 0)
    def _():
        stage_queries(qkv_ref, qpad_ref)
        stage_keys(qkv_ref, kpad_ref, kt_ref)
        filter_keys(kt_ref, thi_ref, tlo_ref, stack_ref, kcat_ref, lags)

    full = bounds_ref[block]
    last = bounds_ref[blocks + block]
    for head in range(2):
        rows = qpad_ref[head, pl.ds(first_row, TILE + ROWPAD), :].astype(jnp.float32)
        qcat_ref[head] = lagged(rows, lags)
        top_ref[head] = jnp.full((TILE, LANES), -1e30, jnp.float32)
        sum_ref[head] = jnp.zeros((TILE, LANES), jnp.float32)
        o_ref[head] = jnp.zeros(o_ref.shape[1:], jnp.float32)

    def full_tiles(first, width):
        for head in range(2):
            logits = dot_nn(qcat_ref[head], kcat_ref[head, :, pl.ds(first, width)])
            c_ref[head, :, pl.ds(first, width)] = logits
            top = top_ref[head]
            for part in range(width // LANES):
                top = jnp.maximum(top, logits[:, part * LANES : (part + 1) * LANES])
            top_ref[head] = top

    over_tiles(full, full_tiles)

    source_rows = first_row - ROWPAD + lax.broadcasted_iota(jnp.int32, (TILE + ROWPAD, 1), 0)
    source_ends = row_ends(source_rows, starts_ref, pics)
    target_rows = first_row + lax.broadcasted_iota(jnp.int32, (TILE, 1), 0)
    target_ends = row_ends(target_rows, starts_ref, pics)

    def mixed_tiles(first, width):
        parts = width // TILE
        columns = first - FRONT + lax.broadcasted_iota(jnp.int32, (1, width + TILE), 1)
        source_allowed = columns <= source_ends
        for head in range(2):
            raw = dot_nn(qpad_ref[head, pl.ds(first_row, TILE + ROWPAD), :], kt_ref[head, :, pl.ds(first, width + TILE)])
            raw = jnp.where(source_allowed, raw, 0.0).astype(jnp.bfloat16)
            stacked = [raw[:, part * TILE : (part + 2) * TILE] for part in range(parts)]
            taps = dot_nn(stacked[0] if parts == 1 else jnp.concatenate(stacked, axis=0), thi_ref[head])
            top = top_ref[head]
            for part in range(parts):
                base = part * (TILE + ROWPAD) + ROWPAD
                logits = taps[base : base + TILE, :TILE]
                for lag in range(1, lags):
                    logits = logits + taps[base - lag : base - lag + TILE, lag * TILE : (lag + 1) * TILE]
                targets = first + part * TILE + lax.broadcasted_iota(jnp.int32, (1, TILE), 1)
                logits = jnp.where(targets <= target_ends, logits, -1e30)
                c_ref[head, :, pl.ds(first + part * TILE, TILE)] = logits
                top = jnp.maximum(top, logits)
            top_ref[head] = top

    over_edges(full, last + 1, mixed_tiles)

    for head in range(2):
        top_ref[head] = jnp.broadcast_to(
            jnp.max(top_ref[head], axis=1, keepdims=True), (TILE, LANES)
        )

    def soft_tiles(first, width):
        for head in range(2):
            parts = []
            total = sum_ref[head]
            for part in range(width // LANES):
                logits = c_ref[head, :, pl.ds(first + part * LANES, LANES)]
                value = jnp.exp(logits - top_ref[head])
                total = total + value
                parts.append(value.astype(jnp.bfloat16))
            sum_ref[head] = total
            weights = parts[0] if len(parts) == 1 else jnp.concatenate(parts, axis=1)
            e_ref[head, :, pl.ds(first, width)] = weights
            o_ref[head] += dot_nn(weights, qkv_ref[pl.ds(first, width), 4 * LANES :])

    over_tiles(last + 1, soft_tiles)

    for head in range(2):
        inverse = 1.0 / jnp.sum(sum_ref[head], axis=1, keepdims=True)
        inv_ref[head] = jnp.broadcast_to(inverse, (TILE, LANES))
        o_ref[head] = o_ref[head] * inverse
    for out_head in range(2):
        lanes = slice(out_head * LANES, (out_head + 1) * LANES)
        weights = [mix_ref[group * 4 + out_head * 2 + head] for head in range(2)]
        normal, _, _ = centre([o_ref[head, :, lanes] for head in range(2)], weights)
        z_ref[:, lanes] = (normal * gain_ref[:, lanes]).astype(jnp.bfloat16)


def fold_rows(values):
    return jnp.sum(values.reshape(TILE // 8, 8, LANES), axis=0)


def backward_kernel(
    bounds_ref, starts_ref, mix_ref, gain_ref, qkv_ref, thi_ref, tlo_ref, ttr_ref,
    e_ref, o_ref, inv_ref, dz_ref, *refs, lags, pics, group,
):
    (
        low_ref, gram_ref, dgain_ref, dmix_ref,
        qpad_ref, kpad_ref, kt_ref, vt_ref, stack_ref, kcat_ref,
        dq_ref, dkt_ref, dvt_ref, dkcat_ref, spread_ref, rowst_ref, dqcat_ref, qcatt_ref, x_ref, xt_ref, delta_ref,
    ) = refs[-21:]
    block = pl.program_id(0)
    blocks = pl.num_programs(0)
    first_row = pl.multiple_of(block * TILE, TILE)

    @pl.when(block == 0)
    def _():
        stage_queries(qkv_ref, qpad_ref)
        stage_keys(qkv_ref, kpad_ref, kt_ref)
        filter_keys(kt_ref, thi_ref, tlo_ref, stack_ref, kcat_ref, lags)

        def tile_step(tile, carry):
            first = pl.multiple_of(tile * TILE, TILE)
            for head in range(2):
                rows = qkv_ref[pl.ds(first, TILE), (4 + head) * LANES : (5 + head) * LANES].astype(jnp.float32)
                vt_ref[head * LANES : (head + 1) * LANES, pl.ds(first, TILE)] = jnp.transpose(rows).astype(jnp.bfloat16)
            return carry

        lax.fori_loop(0, LEN // TILE, tile_step, 0)
        dkcat_ref[...] = jnp.zeros(dkcat_ref.shape, jnp.float32)
        dq_ref[...] = jnp.zeros(dq_ref.shape, jnp.float32)
        dkt_ref[...] = jnp.zeros(dkt_ref.shape, jnp.float32)
        dvt_ref[...] = jnp.zeros(dvt_ref.shape, jnp.float32)
        gram_ref[...] = jnp.zeros(gram_ref.shape, jnp.float32)
        dgain_ref[...] = jnp.zeros(dgain_ref.shape, jnp.float32)
        dmix_ref[...] = jnp.zeros(dmix_ref.shape, jnp.float32)

    full = bounds_ref[block]
    last = bounds_ref[blocks + block]
    out_grads = []
    for out_head in range(2):
        lanes = slice(out_head * LANES, (out_head + 1) * LANES)
        parts = [o_ref[head, :, lanes] for head in range(2)]
        weights = [mix_ref[group * 4 + out_head * 2 + head] for head in range(2)]
        normal, spread, inside = centre(parts, weights)
        grads = dz_ref[:, lanes].astype(jnp.float32)
        dgain_ref[0, :, lanes] += fold_rows(grads * normal)
        grads = grads * gain_ref[:, lanes]
        mean = jnp.sum(grads, axis=1, keepdims=True) / HD
        slope = jnp.sum(grads * normal, axis=1, keepdims=True) / HD
        grads = jnp.where(inside, (grads - mean - normal * slope) * spread, 0.0)
        grads = grads.astype(jnp.bfloat16).astype(jnp.float32)
        for head in range(2):
            dmix_ref[0, 2 * out_head + head] += fold_rows(grads * parts[head])
        out_grads.append(grads)
    for head in range(2):
        rows = qpad_ref[head, pl.ds(first_row, TILE + ROWPAD), :].astype(jnp.float32)
        rowst_ref[head] = jnp.transpose(rows).astype(jnp.bfloat16)
        for lag in range(lags):
            turned = jnp.transpose(rows[ROWPAD - lag : ROWPAD - lag + TILE])
            qcatt_ref[head, lag * HD : (lag + 1) * HD, :] = turned[:HD].astype(jnp.bfloat16)
        dqcat_ref[head] = jnp.zeros(dqcat_ref.shape[1:], jnp.float32)
        inverse = inv_ref[head]
        delta = jnp.zeros((TILE, 1), jnp.float32)
        for out_head in range(2):
            weight = mix_ref[group * 4 + out_head * 2 + head]
            scaled = out_grads[out_head] * (inverse * weight)
            lanes = slice(out_head * LANES, (out_head + 1) * LANES)
            delta = delta + jnp.sum(scaled * o_ref[head, :, lanes], axis=1, keepdims=True)
            x_ref[head, :, lanes] = scaled.astype(jnp.bfloat16)
            xt_ref[head, lanes, :] = jnp.transpose(scaled).astype(jnp.bfloat16)
        delta_ref[head] = jnp.broadcast_to(delta, (TILE, LANES))

    def score_grads(head, first, width):
        prob_grads = dot_nn(x_ref[head], vt_ref[:, pl.ds(first, width)])
        weights = e_ref[head, :, pl.ds(first, width)]
        dvt_ref[:, pl.ds(first, width)] += dot_nn(xt_ref[head], weights)
        delta = delta_ref[head]
        parts = [
            weights[:, part * LANES : (part + 1) * LANES].astype(jnp.float32)
            * (prob_grads[:, part * LANES : (part + 1) * LANES] - delta)
            for part in range(width // LANES)
        ]
        return parts[0] if len(parts) == 1 else jnp.concatenate(parts, axis=1)

    def full_tiles(first, width):
        for head in range(2):
            grads = score_grads(head, first, width).astype(jnp.bfloat16)
            dqcat_ref[head] += dot_nt(grads, kcat_ref[head, :, pl.ds(first, width)])
            filtered = dot_nn(qcatt_ref[head], grads)
            for part in range(width // TILE):
                for lag in range(lags):
                    dkcat_ref[head, first // TILE + part, :HD, lag * TILE : (lag + 1) * TILE] += filtered[
                        lag * HD : (lag + 1) * HD, part * TILE : (part + 1) * TILE
                    ]

    over_tiles(full, full_tiles)

    source_rows = first_row - ROWPAD + lax.broadcasted_iota(jnp.int32, (TILE + ROWPAD, 1), 0)
    source_ends = row_ends(source_rows, starts_ref, pics)
    turned_rows = first_row - ROWPAD + lax.broadcasted_iota(jnp.int32, (1, TILE + ROWPAD), 1)
    turned_ends = row_ends(turned_rows, starts_ref, pics)

    def mixed_tiles(first, width):
        parts = width // TILE
        columns = first - FRONT + lax.broadcasted_iota(jnp.int32, (1, width + TILE), 1)
        turned_columns = first - FRONT + lax.broadcasted_iota(jnp.int32, (width + TILE, 1), 0)
        for head in range(2):
            grads = score_grads(head, first, width)
            above = jnp.zeros((ROWPAD, TILE), jnp.float32)
            below = jnp.zeros((8, TILE), jnp.float32)
            shifted = []
            for part in range(parts):
                padded = jnp.concatenate([above, grads[:, part * TILE : (part + 1) * TILE], below], axis=0)
                shifted.append(
                    jnp.concatenate([padded[lag : lag + TILE + ROWPAD] for lag in range(lags)], axis=1).astype(jnp.bfloat16)
                )
            stacked = shifted[0] if parts == 1 else jnp.concatenate(shifted, axis=0)
            spread = dot_nn(stacked, ttr_ref[head])
            if parts == 2:
                upper = spread[: TILE + ROWPAD]
                lower = spread[TILE + ROWPAD :]
                spread = jnp.concatenate([upper[:, :TILE], upper[:, TILE:] + lower[:, :TILE], lower[:, TILE:]], axis=1)
            raw_grads = jnp.where(columns <= source_ends, spread, 0.0).astype(jnp.bfloat16)
            window = kpad_ref[head, pl.ds(first, width + TILE), :]
            dq_ref[head, pl.ds(first_row, TILE + ROWPAD), :] += dot_nn(raw_grads, window)
            dkt_ref[head, :, pl.ds(first, width + TILE)] += dot_nn(rowst_ref[head], raw_grads)
            turned = dot_nn(window, rowst_ref[head])
            turned = jnp.where(turned_columns <= turned_ends, turned, 0.0).astype(jnp.bfloat16)
            total = dot_nn(turned[: 2 * TILE], shifted[0])
            for part in range(1, parts):
                total = total + dot_nn(turned[part * TILE : (part + 2) * TILE], shifted[part])
            gram_ref[head] += total

    over_edges(full, last + 1, mixed_tiles)

    for head in range(2):
        total = jnp.zeros((TILE + ROWPAD, LANES), jnp.float32)
        for lag in range(lags):
            part = dqcat_ref[head, :, lag * LANES : (lag + 1) * LANES]
            pieces = [jnp.zeros((ROWPAD, LANES), jnp.float32), part, jnp.zeros((8, LANES), jnp.float32)]
            total = total + jnp.concatenate(pieces, axis=0)[lag : lag + TILE + ROWPAD]
        dq_ref[head, pl.ds(first_row, TILE + ROWPAD), :] += total

    @pl.when(block == blocks - 1)
    def _():
        for head in range(2):

            filtered = dkcat_ref[head].reshape(LEN, lags * TILE).astype(jnp.bfloat16)
            windows = dot_nn(filtered, ttr_ref[head])
            for tile in range(LEN // TILE):
                rows = slice(tile * TILE, (tile + 1) * TILE)
                dkt_ref[head, :, tile * TILE : (tile + 2) * TILE] += windows[rows]
                spread_ref[:, rows] = kpad_ref[head, tile * TILE : (tile + 2) * TILE, :]
            gram_ref[head] += dot_nn(spread_ref[...], filtered)
            low_ref[:, head * LANES : (head + 1) * LANES] = dq_ref[head, ROWPAD:, :].astype(jnp.bfloat16)

            def turn_step(tile, carry):
                first = pl.multiple_of(tile * TILE, TILE)
                half = TILE // 2
                lanes = slice((2 + head) * LANES, (3 + head) * LANES)
                front = jnp.transpose(dkt_ref[head, :, pl.ds(first, TILE)]).astype(jnp.bfloat16)
                back = jnp.transpose(dkt_ref[head, :, pl.ds(first + TILE, TILE)]).astype(jnp.bfloat16)
                low_ref[pl.ds(first, half), lanes] = front[half:]
                low_ref[pl.ds(first + half, half), lanes] = back[:half]
                lanes = slice((4 + head) * LANES, (5 + head) * LANES)
                turned = jnp.transpose(dvt_ref[head * LANES : (head + 1) * LANES, pl.ds(first, TILE)])
                low_ref[pl.ds(first, TILE), lanes] = turned.astype(jnp.bfloat16)
                return carry

            lax.fori_loop(0, LEN // TILE, turn_step, 0)


def banded_taps(kernel, scale):
    heads, lags, taps = kernel.shape
    source = lax.broadcasted_iota(jnp.int32, (2 * TILE, TILE), 0)
    target = lax.broadcasted_iota(jnp.int32, (2 * TILE, TILE), 1)
    tap = target + FRONT + taps // 2 - source
    banded = jnp.zeros((heads, 2 * TILE, lags, TILE), jnp.float32)
    for index in range(taps):
        banded = jnp.where(
            (tap == index)[None, :, None, :], (kernel[:, :, index] * scale)[:, None, :, None], banded
        )
    return banded.reshape(heads, 2 * TILE, lags * TILE)


def gather_taps(gram, lags, taps, scale):
    heads = gram.shape[0]
    source = lax.broadcasted_iota(jnp.int32, (2 * TILE, TILE), 0)
    target = lax.broadcasted_iota(jnp.int32, (2 * TILE, TILE), 1)
    tap = target + FRONT + taps // 2 - source
    split = gram.reshape(heads, 2 * TILE, lags, TILE)
    sums = [
        jnp.sum(jnp.where((tap == index)[None, :, None, :], split, 0.0), axis=(1, 3)) for index in range(taps)
    ]
    return jnp.stack(sums, axis=2) * scale


def tile_bounds(starts):
    blocks = LEN // TILE
    firsts = jnp.arange(blocks, dtype=jnp.int32) * TILE
    full = jnp.maximum((row_ends(firsts - 5, starts, starts.shape[0]) - 4) // TILE, 0)
    last = row_ends(firsts + TILE - 1, starts, starts.shape[0]) // TILE
    return jnp.concatenate([full, last])


SMEM = pl.BlockSpec(memory_space=pltpu.SMEM)


def pair_spec(group, *shape):
    return pl.BlockSpec((2,) + shape, lambda block: (group,) + (0,) * len(shape))


def row_spec(*shape):
    return pl.BlockSpec((2,) + shape, lambda block: (0, block) + (0,) * (len(shape) - 1))


def wide_spec(group, rows, width):
    return pl.BlockSpec((rows, width), lambda block: (0, group))


def tile_spec(width):
    return pl.BlockSpec((TILE, width), lambda block: (block, 0))


def attention_forward(group, bounds, starts, mixing, gain, qkv, thi, tlo, lags):
    return pl.pallas_call(
        functools.partial(forward_kernel, lags=lags, pics=starts.shape[0], group=group),
        grid=(LEN // TILE,),
        in_specs=[
            SMEM, SMEM, SMEM,
            wide_spec(group, 1, 2 * LANES),
            wide_spec(group, LEN, 6 * LANES),
            pair_spec(group, 2 * TILE, lags * TILE),
            pair_spec(group, 2 * TILE, lags * TILE),
        ],
        out_specs=[
            row_spec(TILE, LEN), row_spec(TILE, 2 * LANES), row_spec(TILE, LANES),
            tile_spec(2 * LANES),
        ],
        out_shape=[
            jax.ShapeDtypeStruct((2, LEN, LEN), jnp.bfloat16),
            jax.ShapeDtypeStruct((2, LEN, 2 * LANES), jnp.float32),
            jax.ShapeDtypeStruct((2, LEN, LANES), jnp.float32),
            jax.ShapeDtypeStruct((LEN, 2 * LANES), jnp.bfloat16),
        ],
        scratch_shapes=[
            pltpu.VMEM((2, LEN + ROWPAD, LANES), jnp.bfloat16),
            pltpu.VMEM((2, COLS, LANES), jnp.bfloat16),
            pltpu.VMEM((2, LANES, COLS), jnp.bfloat16),
            pltpu.VMEM((LEN, 2 * TILE), jnp.bfloat16),
            pltpu.VMEM((2, lags * LANES, LEN), jnp.bfloat16),
            pltpu.VMEM((2, TILE, LEN), jnp.float32),
            pltpu.VMEM((2, TILE, lags * LANES), jnp.bfloat16),
            pltpu.VMEM((2, TILE, LANES), jnp.float32),
            pltpu.VMEM((2, TILE, LANES), jnp.float32),
        ],
        compiler_params=pltpu.CompilerParams(vmem_limit_bytes=VMEM_BYTES),
        cost_estimate=pl.CostEstimate(flops=70_000_000_000, transcendentals=0, bytes_accessed=20_000_000),
        name="attention_forward",
    )(bounds, starts, mixing.reshape(-1), gain, qkv, thi, tlo)


def attention_backward(group, bounds, starts, mixing, gain, qkv, thi, tlo, ttr, e, o, inv, dz, low, lags):
    width = qkv.shape[1]
    joined = [] if low is None else [low]
    return pl.pallas_call(
        functools.partial(backward_kernel, lags=lags, pics=starts.shape[0], group=group),
        grid=(LEN // TILE,),
        in_specs=[
            SMEM, SMEM, SMEM,
            wide_spec(group, 1, 2 * LANES),
            wide_spec(group, LEN, 6 * LANES),
            pair_spec(group, 2 * TILE, lags * TILE),
            pair_spec(group, 2 * TILE, lags * TILE),
            pair_spec(group, lags * TILE, 2 * TILE),
            row_spec(TILE, LEN), row_spec(TILE, 2 * LANES), row_spec(TILE, LANES),
            tile_spec(2 * LANES),
        ] + [pl.BlockSpec(memory_space=pl.ANY)] * len(joined),
        out_specs=[
            wide_spec(group, LEN, 6 * LANES),
            pair_spec(0, 2 * TILE, lags * TILE),
            pl.BlockSpec((1, 8, 2 * LANES), lambda block: (0, 0, 0)),
            pl.BlockSpec((1, 4, 8, LANES), lambda block: (0, 0, 0, 0)),
        ],
        out_shape=[
            jax.ShapeDtypeStruct((LEN, width), jnp.bfloat16),
            jax.ShapeDtypeStruct((2, 2 * TILE, lags * TILE), jnp.float32),
            jax.ShapeDtypeStruct((1, 8, 2 * LANES), jnp.float32),
            jax.ShapeDtypeStruct((1, 4, 8, LANES), jnp.float32),
        ],
        scratch_shapes=[
            pltpu.VMEM((2, LEN + ROWPAD, LANES), jnp.bfloat16),
            pltpu.VMEM((2, COLS, LANES), jnp.bfloat16),
            pltpu.VMEM((2, LANES, COLS), jnp.bfloat16),
            pltpu.VMEM((2 * LANES, LEN), jnp.bfloat16),
            pltpu.VMEM((LEN, 2 * TILE), jnp.bfloat16),
            pltpu.VMEM((2, lags * LANES, LEN), jnp.bfloat16),
            pltpu.VMEM((2, LEN + ROWPAD, LANES), jnp.float32),
            pltpu.VMEM((2, LANES, COLS), jnp.float32),
            pltpu.VMEM((2 * LANES, LEN), jnp.float32),
            pltpu.VMEM((2, LEN // TILE, LANES, lags * TILE), jnp.float32),
            pltpu.VMEM((2 * TILE, LEN), jnp.bfloat16),
            pltpu.VMEM((2, LANES, TILE + ROWPAD), jnp.bfloat16),
            pltpu.VMEM((2, TILE, lags * LANES), jnp.float32),
            pltpu.VMEM((2, lags * HD, TILE), jnp.bfloat16),
            pltpu.VMEM((2, TILE, 2 * LANES), jnp.bfloat16),
            pltpu.VMEM((2, 2 * LANES, TILE), jnp.bfloat16),
            pltpu.VMEM((2, TILE, LANES), jnp.float32),
        ],
        compiler_params=pltpu.CompilerParams(vmem_limit_bytes=VMEM_BYTES),
        cost_estimate=pl.CostEstimate(flops=115_000_000_000, transcendentals=0, bytes_accessed=20_000_000),
        input_output_aliases={12: 0} if joined else {},
        name="attention_backward",
    )(bounds, starts, mixing.reshape(-1), gain, qkv, thi, tlo, ttr, e, o, inv, dz, *joined)


def pad_heads(columns, heads):
    rows = columns.shape[0]
    split = columns.reshape(rows, heads, HD)
    return jnp.pad(split, ((0, 0), (0, 0), (0, LANES - HD)))


def drop_pads(columns, heads):
    rows = columns.shape[0]
    return columns.reshape(rows, heads, LANES)[:, :, :HD].reshape(rows, heads * HD)


def join_pairs(queries, key_rows, values, heads):
    rows = queries.shape[0]
    parts = [pad_heads(part, heads).reshape(rows, heads // 2, 2, LANES) for part in (queries, key_rows, values)]
    return jnp.stack(parts, axis=2).reshape(rows, heads * 3 * LANES)


def split_pairs(columns, heads):
    rows = columns.shape[0]
    split = columns.reshape(rows, heads // 2, 3, 2, LANES)[..., :HD]
    return [split[:, :, part].reshape(rows, heads * HD) for part in range(3)]


def rms_norm(values, gain):
    return values * lax.rsqrt(jnp.mean(values * values, axis=-1, keepdims=True) + epsilon) * gain


def swiglu(gate, upper):
    return jax.nn.silu(gate) * upper


def shift(values, step):
    size = lax.axis_size("tensor")
    return lax.ppermute(values, "tensor", [(index, (index + step) % size) for index in range(size)])


def swap(values):
    size = lax.axis_size("tensor")
    return lax.ppermute(values, "tensor", [(index, index ^ 1) for index in range(size)])


def line_gather(rows, chunks):
    size = lax.axis_size("tensor")
    index = lax.axis_index("tensor")
    count = rows.shape[0]
    part = count // chunks
    gathered = jnp.zeros((size * count,) + rows.shape[1:], rows.dtype)
    gathered = lax.dynamic_update_slice_in_dim(gathered, rows, index * count, 0)
    rising = [rows[chunk * part : (chunk + 1) * part] for chunk in range(chunks)]
    falling = list(rising)
    from_below, from_above = [], []
    for step in range(1, size):
        upward = [(i, i + 1) for i in range(size - 1) if i >= step - 1]
        downward = [(i + 1, i) for i in range(size - 1) if i + 1 <= size - step]
        for chunk in range(chunks):
            rising[chunk] = lax.ppermute(rising[chunk], "tensor", upward)
            falling[chunk] = lax.ppermute(falling[chunk], "tensor", downward)
        from_below.append(list(rising))
        from_above.append(list(falling))
    for step in range(1, size):
        first = ((index - step) % size) * count
        for chunk in range(chunks):
            piece = jnp.where(index >= step, from_below[step - 1][chunk], from_above[size - step - 1][chunk])
            gathered = lax.dynamic_update_slice_in_dim(gathered, piece, first + chunk * part, 0)
    return gathered


def token_scatter(parts, count):
    size = lax.axis_size("tensor")
    index = lax.axis_index("tensor")
    sums, arrivals = [], []
    for values in parts:

        def block(step):
            return lax.dynamic_slice_in_dim(values, ((index + step) % size) * count, count, 0)

        received = [shift(block(step), step) for step in range(1, size)]
        total = block(0).astype(jnp.float32)
        for part in received:
            total = total + part.astype(jnp.float32)
        sums.append(total)
        arrivals.append(received[0])
    return jnp.concatenate(sums, axis=1), arrivals


def sum_all(values):
    for axis in ("dp", "tensor"):
        size = lax.axis_size(axis)
        step = 1
        while step < size:
            values = values + lax.ppermute(values, axis, [(i, i ^ step) for i in range(size)])
            step *= 2
    return values


def after(values, *others):
    return lax.optimization_barrier((values,) + others)[0]


def shards(
    layer_input,
    piece_starts,
    query_weight,
    key_weight,
    value_weight,
    out_weight,
    gate_weight,
    up_weight,
    down_weight,
    attention_gain,
    feedforward_gain,
    head_gain,
    score_kernel,
    head_mix,
    output_grad,
):
    size = lax.axis_size("tensor")
    index = lax.axis_index("tensor")
    width_local = query_weight.shape[1]
    heads = width_local // HD
    pairs = heads // 2
    wide = 2 * LANES
    hidden_local = gate_weight.shape[1]
    count = layer_input.shape[0]
    lags, taps = score_kernel.shape[1:]
    score_scale = 1.0 / math.sqrt(HD)

    inputs = layer_input.astype(jnp.float32)
    normed, first_pull = jax.vjp(rms_norm, inputs, attention_gain)
    normed_low = normed.astype(jnp.bfloat16)
    rows_all = line_gather(normed_low, 2)

    query_weight, key_weight, value_weight = after((query_weight, key_weight, value_weight), normed_low)
    qkv_full = lax.all_gather(
        join_pairs(query_weight, key_weight, value_weight, heads), "dp", axis=0, tiled=True
    )
    kernel_local = lax.dynamic_slice_in_dim(score_kernel, index * heads, heads, 0)
    mixing_local = lax.dynamic_slice_in_dim(head_mix, index * pairs, pairs, 0)
    gain_local = lax.dynamic_slice_in_dim(head_gain, index * width_local, width_local, 0)
    gain_pad = pad_heads(gain_local[None], heads).reshape(1, heads * LANES)
    starts = piece_starts[0]
    bounds = tile_bounds(starts)
    banded = banded_taps(kernel_local, score_scale)
    taps_high = banded.astype(jnp.bfloat16)
    taps_low = (banded - taps_high.astype(jnp.float32)).astype(jnp.bfloat16)
    taps_turned = taps_high.transpose(0, 2, 1)

    out_own = pad_heads(after(out_weight, rows_all).T, heads).reshape(-1, heads * LANES)
    out_parts = [out_own] + [shift(out_own, step) for step in range(1, size)]
    qkv = dot_nn(rows_all, qkv_full).astype(jnp.bfloat16)
    qkv, taps_high, taps_low, taps_turned, out_parts = lax.optimization_barrier(
        (qkv, taps_high, taps_low, taps_turned, out_parts)
    )
    out_full = lax.all_gather(
        jnp.concatenate(
            [part[:, pair * wide : (pair + 1) * wide] for pair in range(pairs) for part in out_parts], axis=1
        ),
        "dp", axis=0, tiled=True,
    )
    gate_up_own = after(jnp.concatenate([gate_weight, up_weight], axis=1), rows_all)
    down_own = after(down_weight.T, rows_all)
    gate_up = [gate_up_own] + [shift(gate_up_own, step) for step in range(2, size, 2)]
    down = [down_own] + [shift(down_own, step) for step in range(2, size, 2)]
    grads_swapped = swap(after(output_grad, rows_all))

    saved = []
    token_parts = []
    for pair in range(pairs):
        weights, parts_out, inverse, normed_heads = attention_forward(
            pair, bounds, starts, mixing_local, gain_pad, qkv, taps_high, taps_low, lags
        )
        saved.append((weights, parts_out, inverse))
        if pair == 0:
            gate_up, down, grads_swapped = after((gate_up, down, grads_swapped), normed_heads)
        for step in range(size):
            first = ((index + step) % size) * count
            part = lax.dynamic_slice_in_dim(normed_heads, first, count, 0)
            token_parts.append(part if step == 0 else shift(part, step))
    token_heads = jnp.concatenate(token_parts, axis=1)
    grads_two = jnp.concatenate([output_grad, grads_swapped], axis=0)

    gate_up_full = lax.all_gather(
        jnp.concatenate([part[:, :hidden_local] for part in gate_up] + [part[:, hidden_local:] for part in gate_up], axis=1),
        "dp", axis=0, tiled=True,
    )
    down_full = lax.all_gather(jnp.concatenate(down, axis=1), "dp", axis=0, tiled=True)
    hidden_width = down_full.shape[1]
    gate_full = gate_up_full[:, :hidden_width]
    up_full = gate_up_full[:, hidden_width:]

    hidden = inputs + dot_nt(token_heads, out_full)
    ffn_in, second_pull = jax.vjp(rms_norm, hidden, feedforward_gain)
    ffn_low = ffn_in.astype(jnp.bfloat16)
    lead = count // 4 // 16 * 16
    ffn_two = jnp.concatenate([ffn_low, swap(ffn_low)], axis=0)
    halves = (ffn_low, ffn_two[count:])
    gates, uppers, acts = [], [], []
    for rows in halves:
        gates.append(dot_nn(rows, gate_full))
        uppers.append(dot_nn(rows, up_full))
        acts.append(swiglu(gates[-1], uppers[-1]).astype(jnp.bfloat16))
    act_low = jnp.concatenate(acts, axis=0)
    down_part = dot_tn(grads_two, act_low).astype(jnp.bfloat16)
    down_sum = lax.psum_scatter(down_part, "dp", scatter_dimension=0, tiled=True)
    act_grads = dot_nn(after(grads_two, down_part), down_full)
    gate_lows, up_lows = [], []
    for half in range(2):
        gate_grads, up_grads = jax.vjp(swiglu, gates[half], uppers[half])[1](act_grads[half * count : (half + 1) * count])
        gate_lows.append(gate_grads.astype(jnp.bfloat16))
        up_lows.append(up_grads.astype(jnp.bfloat16))

    def ffn_back(gate_low, up_low):
        return dot_nt(gate_low, gate_full) + dot_nt(up_low, up_full)

    ffn_back_sent = ffn_back(gate_lows[1], up_lows[1]).astype(jnp.bfloat16)
    back_lead = swap(ffn_back_sent[:lead])
    back_rest = swap(ffn_back_sent[lead:])
    kept_gate, kept_up = after((gate_lows[0], up_lows[0]), back_lead)
    ffn_back_kept = ffn_back(kept_gate, kept_up)
    ffn_two_later, gate_later, up_later = after((ffn_two, gate_lows, up_lows), ffn_back_kept)
    gate_up_grads = jnp.concatenate(
        [jnp.concatenate(gate_later, axis=0), jnp.concatenate(up_later, axis=0)], axis=1
    )
    gate_up_part = dot_tn(ffn_two_later, gate_up_grads).astype(jnp.bfloat16)
    gate_up_sum = lax.psum_scatter(gate_up_part, "dp", scatter_dimension=0, tiled=True)
    back_other = jnp.concatenate([back_lead, after(back_rest, gate_up_part)], axis=0)
    ffn_in_grad = ffn_back_kept + back_other.astype(jnp.float32)
    hidden_part, feedforward_gain_part = second_pull(ffn_in_grad)
    hidden_grad = output_grad.astype(jnp.float32) + hidden_part
    hidden_low = hidden_grad.astype(jnp.bfloat16)

    head_back = dot_nn(hidden_low, out_full).astype(jnp.bfloat16)
    head_grads = []
    for pair in range(pairs):
        rows = jnp.zeros((LEN, wide), jnp.bfloat16)
        for step in range(size):
            first = (pair * size + step) * wide
            part = head_back[:, first : first + wide]
            part = part if step == 0 else shift(part, -step)
            rows = lax.dynamic_update_slice_in_dim(rows, part, ((index + step) % size) * count, 0)
        head_grads.append(rows)

    act_later, hidden_later = after((act_low, hidden_low), head_back)
    out_part = dot_tn(hidden_later, token_heads).astype(jnp.bfloat16)
    ffn_out_sent = dot_nt(act_later[count:], down_full).astype(jnp.bfloat16)
    ffn_term = dot_nt(act_later[:count], down_full) + swap(ffn_out_sent).astype(jnp.float32)
    layer_output = (hidden + ffn_term).astype(jnp.bfloat16)

    head_grads[0] = after(head_grads[0], out_part, ffn_out_sent)
    def owned(groups, stride):
        joined = jnp.concatenate(groups[0], axis=1).astype(jnp.float32)
        for step in range(1, len(groups)):
            joined = joined + shift(jnp.concatenate(groups[step], axis=1), -step * stride).astype(jnp.float32)
        return joined

    def columns(values, first, width):
        return values[:, first * width : (first + 1) * width]

    low = None
    grams, gain_parts, mixing_parts = [], [], []
    for pair in range(pairs):
        if pair == pairs - 1:
            head_grads[pair], gate_up_sum, down_sum = lax.optimization_barrier(
                (head_grads[pair], gate_up_sum, down_sum)
            )
        low, gram, gain_part, mixing_part = attention_backward(
            pair, bounds, starts, mixing_local, gain_pad, qkv, taps_high, taps_low, taps_turned,
            *saved[pair], head_grads[pair], low, lags,
        )
        if pair == 0:
            out_sum = lax.psum_scatter(after(out_part, gram), "dp", scatter_dimension=0, tiled=True)
        grams.append(gram)
        gain_parts.append(gain_part)
        mixing_parts.append(mixing_part)
    gram = jnp.concatenate(grams, axis=0)
    gain_parts = jnp.concatenate(gain_parts, axis=0)
    mixing_parts = jnp.concatenate(mixing_parts, axis=0)
    parts = hidden_width // hidden_local
    ffn_sum = owned(
        [
            [columns(gate_up_sum, part, hidden_local), columns(gate_up_sum, parts + part, hidden_local),
             columns(down_sum, part, hidden_local)]
            for part in range(parts)
        ],
        2,
    )
    low, ffn_sum, out_sum = lax.optimization_barrier((low, ffn_sum, out_sum))
    gate_grad, up_grad, down_grad = [columns(ffn_sum, part, hidden_local) for part in range(3)]
    down_grad = down_grad.T

    half = qkv_full.shape[0] // 2
    normed_parts = [
        dot_nt(low, qkv_full[chunk * half : (chunk + 1) * half]).astype(jnp.bfloat16) for chunk in range(2)
    ]
    normed_grad, arrivals = token_scatter(normed_parts, count)
    rows_later, low_later, parts_later, gram, gain_parts, mixing_parts = after(
        (rows_all, low, normed_parts, gram, gain_parts, mixing_parts), arrivals[0]
    )
    qkv_part = dot_tn(rows_later, low_later).astype(jnp.bfloat16)
    qkv_sum = lax.psum_scatter(qkv_part, "dp", scatter_dimension=0, tiled=True).astype(jnp.float32)
    attention_gain_part = jnp.concatenate(
        [
            jnp.sum(
                part.astype(jnp.float32) * rows_later[:, chunk * half : (chunk + 1) * half].astype(jnp.float32), axis=0
            )
            for chunk, part in enumerate(parts_later)
        ]
    ) / attention_gain
    input_part = first_pull(normed_grad)[0]
    input_grad = (hidden_grad + input_part).astype(jnp.bfloat16)
    query_grad, key_grad, value_grad = split_pairs(qkv_sum, heads)
    out_sum = after(out_sum, arrivals[1])
    out_total = owned(
        [[columns(out_sum, pair * size + step, wide) for pair in range(pairs)] for step in range(size)], 1
    )
    out_weight_grad = drop_pads(out_total, heads).T

    kernel_part = gather_taps(gram, lags, taps, score_scale)
    mixing_part = jnp.sum(mixing_parts, axis=(2, 3)).reshape(mixing_local.shape)
    head_gain_part = drop_pads(jnp.sum(gain_parts, axis=1).reshape(1, heads * LANES), heads).reshape(-1)

    def placed(part, whole, first):
        return lax.dynamic_update_slice_in_dim(jnp.zeros(whole.shape, jnp.float32), part, first, 0)

    small = (
        attention_gain_part,
        feedforward_gain_part,
        placed(head_gain_part, head_gain, index * width_local),
        placed(kernel_part, score_kernel, index * heads),
        placed(mixing_part, head_mix, index * pairs),
    )
    packed = jnp.concatenate([part.reshape(-1) for part in small])
    packed = jnp.pad(packed, (0, -packed.shape[0] % 1024)).reshape(-1, LANES)
    packed = sum_all(packed).reshape(-1)
    sums = []
    first = 0
    for part in small:
        sums.append(packed[first : first + part.size].reshape(part.shape))
        first += part.size
    return (
        layer_output,
        input_grad,
        query_grad,
        key_grad,
        value_grad,
        out_weight_grad,
        gate_grad,
        up_grad,
        down_grad,
        *sums,
    )


def solution(mesh):
    placed = (
        P(("dp", "tensor"), None),
        P("dp", None),
        P("dp", "tensor"),
        P("dp", "tensor"),
        P("dp", "tensor"),
        P("tensor", "dp"),
        P("dp", "tensor"),
        P("dp", "tensor"),
        P("tensor", "dp"),
        P(),
        P(),
        P(),
        P(),
        P(),
        P(("dp", "tensor"), None),
    )
    return jax.shard_map(
        shards,
        mesh=mesh,
        in_specs=placed,
        out_specs=(
            P(("dp", "tensor"), None),
            P(("dp", "tensor"), None),
            P("dp", "tensor"),
            P("dp", "tensor"),
            P("dp", "tensor"),
            P("tensor", "dp"),
            P("dp", "tensor"),
            P("dp", "tensor"),
            P("tensor", "dp"),
            P(),
            P(),
            P(),
            P(),
            P(),
        ),
        check_vma=False,
    )
```

```python
import functools
import math

import jax
import jax.numpy as jnp
from jax import lax
from jax.experimental import pallas as pl
from jax.experimental.pallas import tpu as pltpu
from jax.sharding import PartitionSpec as P

HD = 96
LEN = 1664
PIC = 256
TILE = 128
LANES = 128
FRONT = 64
ROWPAD = 16
COLS = LEN + 2 * FRONT
GROUP = 8
VMEM_BYTES = 56 * 1024 * 1024
epsilon = 1e-05


def dot_nn(left, right):
    return jnp.dot(left, right, preferred_element_type=jnp.float32)


def dot_nt(left, right):
    return lax.dot_general(left, right, (((1,), (1,)), ((), ())), preferred_element_type=jnp.float32)


def dot_tn(left, right):
    return lax.dot_general(left, right, (((0,), (0,)), ((), ())), preferred_element_type=jnp.float32)


def row_ends(rows, starts_ref, pics):
    ends = rows
    for piece in range(pics):
        first = starts_ref[piece]
        ends = jnp.where((rows >= first) & (rows < first + PIC), first + PIC - 1, ends)
    return ends


def over_tiles(tiles, work):
    def wide_step(group, carry):
        work(pl.multiple_of(group * GROUP * TILE, GROUP * TILE), GROUP * TILE)
        return carry

    lax.fori_loop(0, tiles // GROUP, wide_step, 0)
    left = tiles % GROUP
    size = GROUP // 2
    while size:
        first = tiles - left % (2 * size)

        @pl.when((left // size) % 2 == 1)
        def _():
            work(pl.multiple_of(first * TILE, TILE), size * TILE)

        size //= 2


def over_edges(first, end, work):
    def pair_step(pair, carry):
        work(pl.multiple_of((first + 2 * pair) * TILE, TILE), 2 * TILE)
        return carry

    lax.fori_loop(0, (end - first) // 2, pair_step, 0)

    @pl.when((end - first) % 2 == 1)
    def _():
        work(pl.multiple_of((end - 1) * TILE, TILE), TILE)


def stage_queries(qkv_ref, qpad_ref):
    for head in range(2):
        qpad_ref[head, :ROWPAD, :] = jnp.zeros((ROWPAD, LANES), jnp.bfloat16)
        qpad_ref[head, ROWPAD:, :] = qkv_ref[:, head * LANES : (head + 1) * LANES]


def stage_keys(qkv_ref, kpad_ref, kt_ref):
    for head in range(2):
        kpad_ref[head, :FRONT, :] = jnp.zeros((FRONT, LANES), jnp.bfloat16)
        kpad_ref[head, FRONT + LEN :, :] = jnp.zeros((FRONT, LANES), jnp.bfloat16)
        kpad_ref[head, FRONT : FRONT + LEN, :] = qkv_ref[:, (2 + head) * LANES : (3 + head) * LANES]

        def tile_step(tile, carry):
            first = pl.multiple_of(tile * TILE, TILE)
            rows = kpad_ref[head, pl.ds(first, TILE), :].astype(jnp.float32)
            kt_ref[head, :, pl.ds(first, TILE)] = jnp.transpose(rows).astype(jnp.bfloat16)
            return carry

        lax.fori_loop(0, COLS // TILE, tile_step, 0)


def filter_keys(kt_ref, thi_ref, tlo_ref, stack_ref, kcat_ref, lags):
    tiles = LEN // TILE
    for head in range(2):
        for tile in range(tiles):
            stack_ref[tile * TILE : (tile + 1) * TILE, :] = kt_ref[head, :, tile * TILE : (tile + 2) * TILE]
        for first in range(0, lags, 2):
            width = min(2, lags - first) * TILE
            lanes = slice(first * TILE, first * TILE + width)
            filtered = dot_nn(stack_ref[...], thi_ref[head, :, lanes]) + dot_nn(stack_ref[...], tlo_ref[head, :, lanes])
            for tile in range(tiles):
                for part in range(width // TILE):
                    lag = first + part
                    kcat_ref[head, lag * LANES : (lag + 1) * LANES, tile * TILE : (tile + 1) * TILE] = filtered[
                        tile * TILE : (tile + 1) * TILE, part * TILE : (part + 1) * TILE
                    ].astype(jnp.bfloat16)


def lagged(rows, lags):
    return jnp.concatenate(
        [rows[ROWPAD - lag : ROWPAD - lag + TILE] for lag in range(lags)], axis=1
    ).astype(jnp.bfloat16)


def centre(parts, weights):
    inside = lax.broadcasted_iota(jnp.int32, (TILE, LANES), 1) < HD
    mixed = parts[0] * weights[0] + parts[1] * weights[1]
    mean = jnp.sum(mixed, axis=1, keepdims=True) / HD
    centred = jnp.where(inside, mixed - mean, 0.0)
    spread = lax.rsqrt(jnp.sum(centred * centred, axis=1, keepdims=True) / HD + epsilon)
    return centred * spread, spread, inside


def forward_kernel(
    bounds_ref, starts_ref, mix_ref, gain_ref, qkv_ref, thi_ref, tlo_ref,
    e_ref, o_ref, inv_ref, z_ref,
    qpad_ref, kpad_ref, kt_ref, stack_ref, kcat_ref, c_ref, qcat_ref, top_ref, sum_ref,
    *, lags, pics, group,
):
    block = pl.program_id(0)
    blocks = pl.num_programs(0)
    first_row = pl.multiple_of(block * TILE, TILE)

    @pl.when(block == 0)
    def _():
        stage_queries(qkv_ref, qpad_ref)
        stage_keys(qkv_ref, kpad_ref, kt_ref)
        filter_keys(kt_ref, thi_ref, tlo_ref, stack_ref, kcat_ref, lags)

    full = bounds_ref[block]
    last = bounds_ref[blocks + block]
    for head in range(2):
        rows = qpad_ref[head, pl.ds(first_row, TILE + ROWPAD), :].astype(jnp.float32)
        qcat_ref[head] = lagged(rows, lags)
        top_ref[head] = jnp.full((TILE, LANES), -1e30, jnp.float32)
        sum_ref[head] = jnp.zeros((TILE, LANES), jnp.float32)
        o_ref[head] = jnp.zeros(o_ref.shape[1:], jnp.float32)

    def full_tiles(first, width):
        for head in range(2):
            logits = dot_nn(qcat_ref[head], kcat_ref[head, :, pl.ds(first, width)])
            c_ref[head, :, pl.ds(first, width)] = logits
            top = top_ref[head]
            for part in range(width // LANES):
                top = jnp.maximum(top, logits[:, part * LANES : (part + 1) * LANES])
            top_ref[head] = top

    over_tiles(full, full_tiles)

    source_rows = first_row - ROWPAD + lax.broadcasted_iota(jnp.int32, (TILE + ROWPAD, 1), 0)
    source_ends = row_ends(source_rows, starts_ref, pics)
    target_rows = first_row + lax.broadcasted_iota(jnp.int32, (TILE, 1), 0)
    target_ends = row_ends(target_rows, starts_ref, pics)

    def mixed_tiles(first, width):
        parts = width // TILE
        columns = first - FRONT + lax.broadcasted_iota(jnp.int32, (1, width + TILE), 1)
        source_allowed = columns <= source_ends
        for head in range(2):
            raw = dot_nn(qpad_ref[head, pl.ds(first_row, TILE + ROWPAD), :], kt_ref[head, :, pl.ds(first, width + TILE)])
            raw = jnp.where(source_allowed, raw, 0.0).astype(jnp.bfloat16)
            stacked = [raw[:, part * TILE : (part + 2) * TILE] for part in range(parts)]
            taps = dot_nn(stacked[0] if parts == 1 else jnp.concatenate(stacked, axis=0), thi_ref[head])
            top = top_ref[head]
            for part in range(parts):
                base = part * (TILE + ROWPAD) + ROWPAD
                logits = taps[base : base + TILE, :TILE]
                for lag in range(1, lags):
                    logits = logits + taps[base - lag : base - lag + TILE, lag * TILE : (lag + 1) * TILE]
                targets = first + part * TILE + lax.broadcasted_iota(jnp.int32, (1, TILE), 1)
                logits = jnp.where(targets <= target_ends, logits, -1e30)
                c_ref[head, :, pl.ds(first + part * TILE, TILE)] = logits
                top = jnp.maximum(top, logits)
            top_ref[head] = top

    over_edges(full, last + 1, mixed_tiles)

    for head in range(2):
        top_ref[head] = jnp.broadcast_to(
            jnp.max(top_ref[head], axis=1, keepdims=True), (TILE, LANES)
        )

    def soft_tiles(first, width):
        for head in range(2):
            parts = []
            total = sum_ref[head]
            for part in range(width // LANES):
                logits = c_ref[head, :, pl.ds(first + part * LANES, LANES)]
                value = jnp.exp(logits - top_ref[head])
                total = total + value
                parts.append(value.astype(jnp.bfloat16))
            sum_ref[head] = total
            weights = parts[0] if len(parts) == 1 else jnp.concatenate(parts, axis=1)
            e_ref[head, :, pl.ds(first, width)] = weights
            o_ref[head] += dot_nn(weights, qkv_ref[pl.ds(first, width), 4 * LANES :])

    over_tiles(last + 1, soft_tiles)

    for head in range(2):
        inverse = 1.0 / jnp.sum(sum_ref[head], axis=1, keepdims=True)
        inv_ref[head] = jnp.broadcast_to(inverse, (TILE, LANES))
        o_ref[head] = o_ref[head] * inverse
    for out_head in range(2):
        lanes = slice(out_head * LANES, (out_head + 1) * LANES)
        weights = [mix_ref[group * 4 + out_head * 2 + head] for head in range(2)]
        normal, _, _ = centre([o_ref[head, :, lanes] for head in range(2)], weights)
        z_ref[:, lanes] = (normal * gain_ref[:, lanes]).astype(jnp.bfloat16)


def fold_rows(values):
    return jnp.sum(values.reshape(TILE // 8, 8, LANES), axis=0)


def backward_kernel(
    bounds_ref, starts_ref, mix_ref, gain_ref, qkv_ref, thi_ref, tlo_ref, ttr_ref,
    e_ref, o_ref, inv_ref, dz_ref, *refs, lags, pics, group,
):
    (
        low_ref, gram_ref, dgain_ref, dmix_ref,
        qpad_ref, kpad_ref, kt_ref, vt_ref, stack_ref, kcat_ref,
        dq_ref, dkt_ref, dvt_ref, dkcat_ref, spread_ref, rowst_ref, dqcat_ref, qcatt_ref, x_ref, xt_ref, delta_ref,
    ) = refs[-21:]
    block = pl.program_id(0)
    blocks = pl.num_programs(0)
    first_row = pl.multiple_of(block * TILE, TILE)

    @pl.when(block == 0)
    def _():
        stage_queries(qkv_ref, qpad_ref)
        stage_keys(qkv_ref, kpad_ref, kt_ref)
        filter_keys(kt_ref, thi_ref, tlo_ref, stack_ref, kcat_ref, lags)

        def tile_step(tile, carry):
            first = pl.multiple_of(tile * TILE, TILE)
            for head in range(2):
                rows = qkv_ref[pl.ds(first, TILE), (4 + head) * LANES : (5 + head) * LANES].astype(jnp.float32)
                vt_ref[head * LANES : (head + 1) * LANES, pl.ds(first, TILE)] = jnp.transpose(rows).astype(jnp.bfloat16)
            return carry

        lax.fori_loop(0, LEN // TILE, tile_step, 0)
        dkcat_ref[...] = jnp.zeros(dkcat_ref.shape, jnp.float32)
        dq_ref[...] = jnp.zeros(dq_ref.shape, jnp.float32)
        dkt_ref[...] = jnp.zeros(dkt_ref.shape, jnp.float32)
        dvt_ref[...] = jnp.zeros(dvt_ref.shape, jnp.float32)
        gram_ref[...] = jnp.zeros(gram_ref.shape, jnp.float32)
        dgain_ref[...] = jnp.zeros(dgain_ref.shape, jnp.float32)
        dmix_ref[...] = jnp.zeros(dmix_ref.shape, jnp.float32)

    full = bounds_ref[block]
    last = bounds_ref[blocks + block]
    out_grads = []
    for out_head in range(2):
        lanes = slice(out_head * LANES, (out_head + 1) * LANES)
        parts = [o_ref[head, :, lanes] for head in range(2)]
        weights = [mix_ref[group * 4 + out_head * 2 + head] for head in range(2)]
        normal, spread, inside = centre(parts, weights)
        grads = dz_ref[:, lanes].astype(jnp.float32)
        dgain_ref[0, :, lanes] += fold_rows(grads * normal)
        grads = grads * gain_ref[:, lanes]
        mean = jnp.sum(grads, axis=1, keepdims=True) / HD
        slope = jnp.sum(grads * normal, axis=1, keepdims=True) / HD
        grads = jnp.where(inside, (grads - mean - normal * slope) * spread, 0.0)
        grads = grads.astype(jnp.bfloat16).astype(jnp.float32)
        for head in range(2):
            dmix_ref[0, 2 * out_head + head] += fold_rows(grads * parts[head])
        out_grads.append(grads)
    for head in range(2):
        rows = qpad_ref[head, pl.ds(first_row, TILE + ROWPAD), :].astype(jnp.float32)
        rowst_ref[head] = jnp.transpose(rows).astype(jnp.bfloat16)
        for lag in range(lags):
            turned = jnp.transpose(rows[ROWPAD - lag : ROWPAD - lag + TILE])
            qcatt_ref[head, lag * HD : (lag + 1) * HD, :] = turned[:HD].astype(jnp.bfloat16)
        dqcat_ref[head] = jnp.zeros(dqcat_ref.shape[1:], jnp.float32)
        inverse = inv_ref[head]
        delta = jnp.zeros((TILE, 1), jnp.float32)
        for out_head in range(2):
            weight = mix_ref[group * 4 + out_head * 2 + head]
            scaled = out_grads[out_head] * (inverse * weight)
            lanes = slice(out_head * LANES, (out_head + 1) * LANES)
            delta = delta + jnp.sum(scaled * o_ref[head, :, lanes], axis=1, keepdims=True)
            x_ref[head, :, lanes] = scaled.astype(jnp.bfloat16)
            xt_ref[head, lanes, :] = jnp.transpose(scaled).astype(jnp.bfloat16)
        delta_ref[head] = jnp.broadcast_to(delta, (TILE, LANES))

    def score_grads(head, first, width):
        prob_grads = dot_nn(x_ref[head], vt_ref[:, pl.ds(first, width)])
        weights = e_ref[head, :, pl.ds(first, width)]
        dvt_ref[:, pl.ds(first, width)] += dot_nn(xt_ref[head], weights)
        delta = delta_ref[head]
        parts = [
            weights[:, part * LANES : (part + 1) * LANES].astype(jnp.float32)
            * (prob_grads[:, part * LANES : (part + 1) * LANES] - delta)
            for part in range(width // LANES)
        ]
        return parts[0] if len(parts) == 1 else jnp.concatenate(parts, axis=1)

    def full_tiles(first, width):
        for head in range(2):
            grads = score_grads(head, first, width).astype(jnp.bfloat16)
            dqcat_ref[head] += dot_nt(grads, kcat_ref[head, :, pl.ds(first, width)])
            filtered = dot_nn(qcatt_ref[head], grads)
            for part in range(width // TILE):
                for lag in range(lags):
                    dkcat_ref[head, first // TILE + part, :HD, lag * TILE : (lag + 1) * TILE] += filtered[
                        lag * HD : (lag + 1) * HD, part * TILE : (part + 1) * TILE
                    ]

    over_tiles(full, full_tiles)

    source_rows = first_row - ROWPAD + lax.broadcasted_iota(jnp.int32, (TILE + ROWPAD, 1), 0)
    source_ends = row_ends(source_rows, starts_ref, pics)
    turned_rows = first_row - ROWPAD + lax.broadcasted_iota(jnp.int32, (1, TILE + ROWPAD), 1)
    turned_ends = row_ends(turned_rows, starts_ref, pics)

    def mixed_tiles(first, width):
        parts = width // TILE
        columns = first - FRONT + lax.broadcasted_iota(jnp.int32, (1, width + TILE), 1)
        turned_columns = first - FRONT + lax.broadcasted_iota(jnp.int32, (width + TILE, 1), 0)
        for head in range(2):
            grads = score_grads(head, first, width)
            above = jnp.zeros((ROWPAD, TILE), jnp.float32)
            below = jnp.zeros((8, TILE), jnp.float32)
            shifted = []
            for part in range(parts):
                padded = jnp.concatenate([above, grads[:, part * TILE : (part + 1) * TILE], below], axis=0)
                shifted.append(
                    jnp.concatenate([padded[lag : lag + TILE + ROWPAD] for lag in range(lags)], axis=1).astype(jnp.bfloat16)
                )
            stacked = shifted[0] if parts == 1 else jnp.concatenate(shifted, axis=0)
            spread = dot_nn(stacked, ttr_ref[head])
            if parts == 2:
                upper = spread[: TILE + ROWPAD]
                lower = spread[TILE + ROWPAD :]
                spread = jnp.concatenate([upper[:, :TILE], upper[:, TILE:] + lower[:, :TILE], lower[:, TILE:]], axis=1)
            raw_grads = jnp.where(columns <= source_ends, spread, 0.0).astype(jnp.bfloat16)
            window = kpad_ref[head, pl.ds(first, width + TILE), :]
            dq_ref[head, pl.ds(first_row, TILE + ROWPAD), :] += dot_nn(raw_grads, window)
            dkt_ref[head, :, pl.ds(first, width + TILE)] += dot_nn(rowst_ref[head], raw_grads)
            turned = dot_nn(window, rowst_ref[head])
            turned = jnp.where(turned_columns <= turned_ends, turned, 0.0).astype(jnp.bfloat16)
            total = dot_nn(turned[: 2 * TILE], shifted[0])
            for part in range(1, parts):
                total = total + dot_nn(turned[part * TILE : (part + 2) * TILE], shifted[part])
            gram_ref[head] += total

    over_edges(full, last + 1, mixed_tiles)

    for head in range(2):
        total = jnp.zeros((TILE + ROWPAD, LANES), jnp.float32)
        for lag in range(lags):
            part = dqcat_ref[head, :, lag * LANES : (lag + 1) * LANES]
            pieces = [jnp.zeros((ROWPAD, LANES), jnp.float32), part, jnp.zeros((8, LANES), jnp.float32)]
            total = total + jnp.concatenate(pieces, axis=0)[lag : lag + TILE + ROWPAD]
        dq_ref[head, pl.ds(first_row, TILE + ROWPAD), :] += total

    @pl.when(block == blocks - 1)
    def _():
        for head in range(2):

            filtered = dkcat_ref[head].reshape(LEN, lags * TILE).astype(jnp.bfloat16)
            windows = dot_nn(filtered, ttr_ref[head])
            for tile in range(LEN // TILE):
                rows = slice(tile * TILE, (tile + 1) * TILE)
                dkt_ref[head, :, tile * TILE : (tile + 2) * TILE] += windows[rows]
                spread_ref[:, rows] = kpad_ref[head, tile * TILE : (tile + 2) * TILE, :]
            gram_ref[head] += dot_nn(spread_ref[...], filtered)
            low_ref[:, head * LANES : (head + 1) * LANES] = dq_ref[head, ROWPAD:, :].astype(jnp.bfloat16)

            def turn_step(tile, carry):
                first = pl.multiple_of(tile * TILE, TILE)
                half = TILE // 2
                lanes = slice((2 + head) * LANES, (3 + head) * LANES)
                front = jnp.transpose(dkt_ref[head, :, pl.ds(first, TILE)]).astype(jnp.bfloat16)
                back = jnp.transpose(dkt_ref[head, :, pl.ds(first + TILE, TILE)]).astype(jnp.bfloat16)
                low_ref[pl.ds(first, half), lanes] = front[half:]
                low_ref[pl.ds(first + half, half), lanes] = back[:half]
                lanes = slice((4 + head) * LANES, (5 + head) * LANES)
                turned = jnp.transpose(dvt_ref[head * LANES : (head + 1) * LANES, pl.ds(first, TILE)])
                low_ref[pl.ds(first, TILE), lanes] = turned.astype(jnp.bfloat16)
                return carry

            lax.fori_loop(0, LEN // TILE, turn_step, 0)


def banded_taps(kernel, scale):
    heads, lags, taps = kernel.shape
    source = lax.broadcasted_iota(jnp.int32, (2 * TILE, TILE), 0)
    target = lax.broadcasted_iota(jnp.int32, (2 * TILE, TILE), 1)
    tap = target + FRONT + taps // 2 - source
    banded = jnp.zeros((heads, 2 * TILE, lags, TILE), jnp.float32)
    for index in range(taps):
        banded = jnp.where(
            (tap == index)[None, :, None, :], (kernel[:, :, index] * scale)[:, None, :, None], banded
        )
    return banded.reshape(heads, 2 * TILE, lags * TILE)


def gather_taps(gram, lags, taps, scale):
    heads = gram.shape[0]
    source = lax.broadcasted_iota(jnp.int32, (2 * TILE, TILE), 0)
    target = lax.broadcasted_iota(jnp.int32, (2 * TILE, TILE), 1)
    tap = target + FRONT + taps // 2 - source
    split = gram.reshape(heads, 2 * TILE, lags, TILE)
    sums = [
        jnp.sum(jnp.where((tap == index)[None, :, None, :], split, 0.0), axis=(1, 3)) for index in range(taps)
    ]
    return jnp.stack(sums, axis=2) * scale


def tile_bounds(starts):
    blocks = LEN // TILE
    firsts = jnp.arange(blocks, dtype=jnp.int32) * TILE
    full = jnp.maximum((row_ends(firsts - 5, starts, starts.shape[0]) - 4) // TILE, 0)
    last = row_ends(firsts + TILE - 1, starts, starts.shape[0]) // TILE
    return jnp.concatenate([full, last])


SMEM = pl.BlockSpec(memory_space=pltpu.SMEM)


def pair_spec(group, *shape):
    return pl.BlockSpec((2,) + shape, lambda block: (group,) + (0,) * len(shape))


def row_spec(*shape):
    return pl.BlockSpec((2,) + shape, lambda block: (0, block) + (0,) * (len(shape) - 1))


def wide_spec(group, rows, width):
    return pl.BlockSpec((rows, width), lambda block: (0, group))


def tile_spec(width):
    return pl.BlockSpec((TILE, width), lambda block: (block, 0))


def attention_forward(group, bounds, starts, mixing, gain, qkv, thi, tlo, lags):
    return pl.pallas_call(
        functools.partial(forward_kernel, lags=lags, pics=starts.shape[0], group=group),
        grid=(LEN // TILE,),
        in_specs=[
            SMEM, SMEM, SMEM,
            wide_spec(group, 1, 2 * LANES),
            wide_spec(group, LEN, 6 * LANES),
            pair_spec(group, 2 * TILE, lags * TILE),
            pair_spec(group, 2 * TILE, lags * TILE),
        ],
        out_specs=[
            row_spec(TILE, LEN), row_spec(TILE, 2 * LANES), row_spec(TILE, LANES),
            tile_spec(2 * LANES),
        ],
        out_shape=[
            jax.ShapeDtypeStruct((2, LEN, LEN), jnp.bfloat16),
            jax.ShapeDtypeStruct((2, LEN, 2 * LANES), jnp.float32),
            jax.ShapeDtypeStruct((2, LEN, LANES), jnp.float32),
            jax.ShapeDtypeStruct((LEN, 2 * LANES), jnp.bfloat16),
        ],
        scratch_shapes=[
            pltpu.VMEM((2, LEN + ROWPAD, LANES), jnp.bfloat16),
            pltpu.VMEM((2, COLS, LANES), jnp.bfloat16),
            pltpu.VMEM((2, LANES, COLS), jnp.bfloat16),
            pltpu.VMEM((LEN, 2 * TILE), jnp.bfloat16),
            pltpu.VMEM((2, lags * LANES, LEN), jnp.bfloat16),
            pltpu.VMEM((2, TILE, LEN), jnp.float32),
            pltpu.VMEM((2, TILE, lags * LANES), jnp.bfloat16),
            pltpu.VMEM((2, TILE, LANES), jnp.float32),
            pltpu.VMEM((2, TILE, LANES), jnp.float32),
        ],
        compiler_params=pltpu.CompilerParams(vmem_limit_bytes=VMEM_BYTES),
        cost_estimate=pl.CostEstimate(flops=70_000_000_000, transcendentals=0, bytes_accessed=20_000_000),
        name="attention_forward",
    )(bounds, starts, mixing.reshape(-1), gain, qkv, thi, tlo)


def attention_backward(group, bounds, starts, mixing, gain, qkv, thi, tlo, ttr, e, o, inv, dz, low, lags):
    width = qkv.shape[1]
    joined = [] if low is None else [low]
    return pl.pallas_call(
        functools.partial(backward_kernel, lags=lags, pics=starts.shape[0], group=group),
        grid=(LEN // TILE,),
        in_specs=[
            SMEM, SMEM, SMEM,
            wide_spec(group, 1, 2 * LANES),
            wide_spec(group, LEN, 6 * LANES),
            pair_spec(group, 2 * TILE, lags * TILE),
            pair_spec(group, 2 * TILE, lags * TILE),
            pair_spec(group, lags * TILE, 2 * TILE),
            row_spec(TILE, LEN), row_spec(TILE, 2 * LANES), row_spec(TILE, LANES),
            tile_spec(2 * LANES),
        ] + [pl.BlockSpec(memory_space=pl.ANY)] * len(joined),
        out_specs=[
            wide_spec(group, LEN, 6 * LANES),
            pair_spec(0, 2 * TILE, lags * TILE),
            pl.BlockSpec((1, 8, 2 * LANES), lambda block: (0, 0, 0)),
            pl.BlockSpec((1, 4, 8, LANES), lambda block: (0, 0, 0, 0)),
        ],
        out_shape=[
            jax.ShapeDtypeStruct((LEN, width), jnp.bfloat16),
            jax.ShapeDtypeStruct((2, 2 * TILE, lags * TILE), jnp.float32),
            jax.ShapeDtypeStruct((1, 8, 2 * LANES), jnp.float32),
            jax.ShapeDtypeStruct((1, 4, 8, LANES), jnp.float32),
        ],
        scratch_shapes=[
            pltpu.VMEM((2, LEN + ROWPAD, LANES), jnp.bfloat16),
            pltpu.VMEM((2, COLS, LANES), jnp.bfloat16),
            pltpu.VMEM((2, LANES, COLS), jnp.bfloat16),
            pltpu.VMEM((2 * LANES, LEN), jnp.bfloat16),
            pltpu.VMEM((LEN, 2 * TILE), jnp.bfloat16),
            pltpu.VMEM((2, lags * LANES, LEN), jnp.bfloat16),
            pltpu.VMEM((2, LEN + ROWPAD, LANES), jnp.float32),
            pltpu.VMEM((2, LANES, COLS), jnp.float32),
            pltpu.VMEM((2 * LANES, LEN), jnp.float32),
            pltpu.VMEM((2, LEN // TILE, LANES, lags * TILE), jnp.float32),
            pltpu.VMEM((2 * TILE, LEN), jnp.bfloat16),
            pltpu.VMEM((2, LANES, TILE + ROWPAD), jnp.bfloat16),
            pltpu.VMEM((2, TILE, lags * LANES), jnp.float32),
            pltpu.VMEM((2, lags * HD, TILE), jnp.bfloat16),
            pltpu.VMEM((2, TILE, 2 * LANES), jnp.bfloat16),
            pltpu.VMEM((2, 2 * LANES, TILE), jnp.bfloat16),
            pltpu.VMEM((2, TILE, LANES), jnp.float32),
        ],
        compiler_params=pltpu.CompilerParams(vmem_limit_bytes=VMEM_BYTES),
        cost_estimate=pl.CostEstimate(flops=115_000_000_000, transcendentals=0, bytes_accessed=20_000_000),
        input_output_aliases={12: 0} if joined else {},
        name="attention_backward",
    )(bounds, starts, mixing.reshape(-1), gain, qkv, thi, tlo, ttr, e, o, inv, dz, *joined)


def pad_heads(columns, heads):
    rows = columns.shape[0]
    split = columns.reshape(rows, heads, HD)
    return jnp.pad(split, ((0, 0), (0, 0), (0, LANES - HD)))


def drop_pads(columns, heads):
    rows = columns.shape[0]
    return columns.reshape(rows, heads, LANES)[:, :, :HD].reshape(rows, heads * HD)


def join_pairs(queries, key_rows, values, heads):
    rows = queries.shape[0]
    parts = [pad_heads(part, heads).reshape(rows, heads // 2, 2, LANES) for part in (queries, key_rows, values)]
    return jnp.stack(parts, axis=2).reshape(rows, heads * 3 * LANES)


def split_pairs(columns, heads):
    rows = columns.shape[0]
    split = columns.reshape(rows, heads // 2, 3, 2, LANES)[..., :HD]
    return [split[:, :, part].reshape(rows, heads * HD) for part in range(3)]


def rms_norm(values, gain):
    return values * lax.rsqrt(jnp.mean(values * values, axis=-1, keepdims=True) + epsilon) * gain


def swiglu(gate, upper):
    return jax.nn.silu(gate) * upper


def shift(values, step):
    size = lax.axis_size("tensor")
    return lax.ppermute(values, "tensor", [(index, (index + step) % size) for index in range(size)])


def swap(values):
    size = lax.axis_size("tensor")
    return lax.ppermute(values, "tensor", [(index, index ^ 1) for index in range(size)])


def line_gather(rows, chunks):
    size = lax.axis_size("tensor")
    index = lax.axis_index("tensor")
    count = rows.shape[0]
    part = count // chunks
    gathered = jnp.zeros((size * count,) + rows.shape[1:], rows.dtype)
    gathered = lax.dynamic_update_slice_in_dim(gathered, rows, index * count, 0)
    rising = [rows[chunk * part : (chunk + 1) * part] for chunk in range(chunks)]
    falling = list(rising)
    from_below, from_above = [], []
    for step in range(1, size):
        upward = [(i, i + 1) for i in range(size - 1) if i >= step - 1]
        downward = [(i + 1, i) for i in range(size - 1) if i + 1 <= size - step]
        for chunk in range(chunks):
            rising[chunk] = lax.ppermute(rising[chunk], "tensor", upward)
            falling[chunk] = lax.ppermute(falling[chunk], "tensor", downward)
        from_below.append(list(rising))
        from_above.append(list(falling))
    for step in range(1, size):
        first = ((index - step) % size) * count
        for chunk in range(chunks):
            piece = jnp.where(index >= step, from_below[step - 1][chunk], from_above[size - step - 1][chunk])
            gathered = lax.dynamic_update_slice_in_dim(gathered, piece, first + chunk * part, 0)
    return gathered


def token_scatter(parts, count):
    size = lax.axis_size("tensor")
    index = lax.axis_index("tensor")
    sums, arrivals = [], []
    for values in parts:

        def block(step):
            return lax.dynamic_slice_in_dim(values, ((index + step) % size) * count, count, 0)

        received = [shift(block(step), step) for step in range(1, size)]
        total = block(0).astype(jnp.float32)
        for part in received:
            total = total + part.astype(jnp.float32)
        sums.append(total)
        arrivals.append(received[0])
    return jnp.concatenate(sums, axis=1), arrivals


def sum_all(values):
    for axis in ("dp", "tensor"):
        size = lax.axis_size(axis)
        step = 1
        while step < size:
            values = values + lax.ppermute(values, axis, [(i, i ^ step) for i in range(size)])
            step *= 2
    return values


def after(values, *others):
    return lax.optimization_barrier((values,) + others)[0]


def shards(
    layer_input,
    piece_starts,
    query_weight,
    key_weight,
    value_weight,
    out_weight,
    gate_weight,
    up_weight,
    down_weight,
    attention_gain,
    feedforward_gain,
    head_gain,
    score_kernel,
    head_mix,
    output_grad,
):
    size = lax.axis_size("tensor")
    index = lax.axis_index("tensor")
    width_local = query_weight.shape[1]
    heads = width_local // HD
    pairs = heads // 2
    wide = 2 * LANES
    hidden_local = gate_weight.shape[1]
    count = layer_input.shape[0]
    lags, taps = score_kernel.shape[1:]
    score_scale = 1.0 / math.sqrt(HD)

    inputs = layer_input.astype(jnp.float32)
    normed, first_pull = jax.vjp(rms_norm, inputs, attention_gain)
    normed_low = normed.astype(jnp.bfloat16)
    rows_all = line_gather(normed_low, 2)

    query_weight, key_weight, value_weight = after((query_weight, key_weight, value_weight), normed_low)
    qkv_full = lax.all_gather(
        join_pairs(query_weight, key_weight, value_weight, heads), "dp", axis=0, tiled=True
    )
    kernel_local = lax.dynamic_slice_in_dim(score_kernel, index * heads, heads, 0)
    mixing_local = lax.dynamic_slice_in_dim(head_mix, index * pairs, pairs, 0)
    gain_local = lax.dynamic_slice_in_dim(head_gain, index * width_local, width_local, 0)
    gain_pad = pad_heads(gain_local[None], heads).reshape(1, heads * LANES)
    starts = piece_starts[0]
    bounds = tile_bounds(starts)
    banded = banded_taps(kernel_local, score_scale)
    taps_high = banded.astype(jnp.bfloat16)
    taps_low = (banded - taps_high.astype(jnp.float32)).astype(jnp.bfloat16)
    taps_turned = taps_high.transpose(0, 2, 1)

    out_own = pad_heads(after(out_weight, rows_all).T, heads).reshape(-1, heads * LANES)
    out_parts = [out_own] + [shift(out_own, step) for step in range(1, size)]
    qkv = dot_nn(rows_all, qkv_full).astype(jnp.bfloat16)
    qkv, taps_high, taps_low, taps_turned, out_parts = lax.optimization_barrier(
        (qkv, taps_high, taps_low, taps_turned, out_parts)
    )
    out_full = lax.all_gather(
        jnp.concatenate(
            [part[:, pair * wide : (pair + 1) * wide] for pair in range(pairs) for part in out_parts], axis=1
        ),
        "dp", axis=0, tiled=True,
    )
    gate_up_own = after(jnp.concatenate([gate_weight, up_weight], axis=1), rows_all)
    down_own = after(down_weight.T, rows_all)
    gate_up = [gate_up_own] + [shift(gate_up_own, step) for step in range(2, size, 2)]
    down = [down_own] + [shift(down_own, step) for step in range(2, size, 2)]
    grads_swapped = swap(after(output_grad, rows_all))

    saved = []
    token_parts = []
    for pair in range(pairs):
        weights, parts_out, inverse, normed_heads = attention_forward(
            pair, bounds, starts, mixing_local, gain_pad, qkv, taps_high, taps_low, lags
        )
        saved.append((weights, parts_out, inverse))
        if pair == 0:
            gate_up, down, grads_swapped = after((gate_up, down, grads_swapped), normed_heads)
        for step in range(size):
            first = ((index + step) % size) * count
            part = lax.dynamic_slice_in_dim(normed_heads, first, count, 0)
            token_parts.append(part if step == 0 else shift(part, step))
    token_heads = jnp.concatenate(token_parts, axis=1)
    grads_two = jnp.concatenate([output_grad, grads_swapped], axis=0)

    gate_up_full = lax.all_gather(
        jnp.concatenate([part[:, :hidden_local] for part in gate_up] + [part[:, hidden_local:] for part in gate_up], axis=1),
        "dp", axis=0, tiled=True,
    )
    down_full = lax.all_gather(jnp.concatenate(down, axis=1), "dp", axis=0, tiled=True)
    hidden_width = down_full.shape[1]
    gate_full = gate_up_full[:, :hidden_width]
    up_full = gate_up_full[:, hidden_width:]

    hidden = inputs + dot_nt(token_heads, out_full)
    ffn_in, second_pull = jax.vjp(rms_norm, hidden, feedforward_gain)
    ffn_low = ffn_in.astype(jnp.bfloat16)
    lead = count // 4 // 16 * 16
    ffn_two = jnp.concatenate([ffn_low, swap(ffn_low)], axis=0)
    halves = (ffn_low, ffn_two[count:])
    gates, uppers, acts = [], [], []
    for rows in halves:
        gates.append(dot_nn(rows, gate_full))
        uppers.append(dot_nn(rows, up_full))
        acts.append(swiglu(gates[-1], uppers[-1]).astype(jnp.bfloat16))
    act_low = jnp.concatenate(acts, axis=0)
    down_part = dot_tn(grads_two, act_low).astype(jnp.bfloat16)
    down_sum = lax.psum_scatter(down_part, "dp", scatter_dimension=0, tiled=True)
    act_grads = dot_nn(after(grads_two, down_part), down_full)
    gate_lows, up_lows = [], []
    for half in range(2):
        gate_grads, up_grads = jax.vjp(swiglu, gates[half], uppers[half])[1](act_grads[half * count : (half + 1) * count])
        gate_lows.append(gate_grads.astype(jnp.bfloat16))
        up_lows.append(up_grads.astype(jnp.bfloat16))

    def ffn_back(gate_low, up_low):
        return dot_nt(gate_low, gate_full) + dot_nt(up_low, up_full)

    ffn_back_sent = ffn_back(gate_lows[1], up_lows[1]).astype(jnp.bfloat16)
    back_lead = swap(ffn_back_sent[:lead])
    back_rest = swap(ffn_back_sent[lead:])
    kept_gate, kept_up = after((gate_lows[0], up_lows[0]), back_lead)
    ffn_back_kept = ffn_back(kept_gate, kept_up)
    ffn_two_later, gate_later, up_later = after((ffn_two, gate_lows, up_lows), ffn_back_kept)
    gate_up_grads = jnp.concatenate(
        [jnp.concatenate(gate_later, axis=0), jnp.concatenate(up_later, axis=0)], axis=1
    )
    gate_up_part = dot_tn(ffn_two_later, gate_up_grads).astype(jnp.bfloat16)
    gate_up_sum = lax.psum_scatter(gate_up_part, "dp", scatter_dimension=0, tiled=True)
    back_other = jnp.concatenate([back_lead, after(back_rest, gate_up_part)], axis=0)
    ffn_in_grad = ffn_back_kept + back_other.astype(jnp.float32)
    hidden_part, feedforward_gain_part = second_pull(ffn_in_grad)
    hidden_grad = output_grad.astype(jnp.float32) + hidden_part
    hidden_low = hidden_grad.astype(jnp.bfloat16)

    head_back = dot_nn(hidden_low, out_full).astype(jnp.bfloat16)
    head_grads = []
    for pair in range(pairs):
        rows = jnp.zeros((LEN, wide), jnp.bfloat16)
        for step in range(size):
            first = (pair * size + step) * wide
            part = head_back[:, first : first + wide]
            part = part if step == 0 else shift(part, -step)
            rows = lax.dynamic_update_slice_in_dim(rows, part, ((index + step) % size) * count, 0)
        head_grads.append(rows)

    act_later, hidden_later = after((act_low, hidden_low), head_back)
    out_part = dot_tn(hidden_later, token_heads).astype(jnp.bfloat16)
    ffn_out_sent = dot_nt(act_later[count:], down_full).astype(jnp.bfloat16)
    ffn_out_other = swap(ffn_out_sent)

    head_grads[0] = after(head_grads[0], out_part, ffn_out_sent)
    def owned(groups, stride):
        joined = jnp.concatenate(groups[0], axis=1).astype(jnp.float32)
        for step in range(1, len(groups)):
            joined = joined + shift(jnp.concatenate(groups[step], axis=1), -step * stride).astype(jnp.float32)
        return joined

    def columns(values, first, width):
        return values[:, first * width : (first + 1) * width]

    low = None
    grams, gain_parts, mixing_parts = [], [], []
    for pair in range(pairs):
        if pair == pairs - 1:
            head_grads[pair], gate_up_sum, down_sum = lax.optimization_barrier(
                (head_grads[pair], gate_up_sum, down_sum)
            )
        low, gram, gain_part, mixing_part = attention_backward(
            pair, bounds, starts, mixing_local, gain_pad, qkv, taps_high, taps_low, taps_turned,
            *saved[pair], head_grads[pair], low, lags,
        )
        if pair == 0:
            out_sum = lax.psum_scatter(after(out_part, gram), "dp", scatter_dimension=0, tiled=True)
        grams.append(gram)
        gain_parts.append(gain_part)
        mixing_parts.append(mixing_part)
    gram = jnp.concatenate(grams, axis=0)
    gain_parts = jnp.concatenate(gain_parts, axis=0)
    mixing_parts = jnp.concatenate(mixing_parts, axis=0)
    parts = hidden_width // hidden_local
    ffn_sum = owned(
        [
            [columns(gate_up_sum, part, hidden_local), columns(gate_up_sum, parts + part, hidden_local),
             columns(down_sum, part, hidden_local)]
            for part in range(parts)
        ],
        2,
    )
    low, ffn_sum, out_sum = lax.optimization_barrier((low, ffn_sum, out_sum))
    gate_grad, up_grad, down_grad = [columns(ffn_sum, part, hidden_local) for part in range(3)]
    down_grad = down_grad.T

    half = qkv_full.shape[0] // 2
    normed_parts = [
        dot_nt(low, qkv_full[chunk * half : (chunk + 1) * half]).astype(jnp.bfloat16) for chunk in range(2)
    ]
    normed_grad, arrivals = token_scatter(normed_parts, count)
    rows_later, low_later, parts_later, gram, gain_parts, mixing_parts = after(
        (rows_all, low, normed_parts, gram, gain_parts, mixing_parts), arrivals[0], arrivals[1]
    )
    qkv_part = dot_tn(rows_later, low_later).astype(jnp.bfloat16)
    qkv_sum = lax.psum_scatter(qkv_part, "dp", scatter_dimension=0, tiled=True).astype(jnp.float32)
    attention_gain_part = jnp.concatenate(
        [
            jnp.sum(
                part.astype(jnp.float32) * rows_later[:, chunk * half : (chunk + 1) * half].astype(jnp.float32), axis=0
            )
            for chunk, part in enumerate(parts_later)
        ]
    ) / attention_gain
    input_part = first_pull(normed_grad)[0]
    input_grad = (hidden_grad + input_part).astype(jnp.bfloat16)
    query_grad, key_grad, value_grad = split_pairs(qkv_sum, heads)
    out_sum = after(out_sum, arrivals[1])
    act_last, ffn_out_other = after((act_low[:count], ffn_out_other), attention_gain_part)
    ffn_term = dot_nt(act_last, down_full) + ffn_out_other.astype(jnp.float32)
    layer_output = (hidden + ffn_term).astype(jnp.bfloat16)
    out_total = owned(
        [[columns(out_sum, pair * size + step, wide) for pair in range(pairs)] for step in range(size)], 1
    )
    out_weight_grad = drop_pads(out_total, heads).T

    kernel_part = gather_taps(gram, lags, taps, score_scale)
    mixing_part = jnp.sum(mixing_parts, axis=(2, 3)).reshape(mixing_local.shape)
    head_gain_part = drop_pads(jnp.sum(gain_parts, axis=1).reshape(1, heads * LANES), heads).reshape(-1)

    def placed(part, whole, first):
        return lax.dynamic_update_slice_in_dim(jnp.zeros(whole.shape, jnp.float32), part, first, 0)

    small = (
        attention_gain_part,
        feedforward_gain_part,
        placed(head_gain_part, head_gain, index * width_local),
        placed(kernel_part, score_kernel, index * heads),
        placed(mixing_part, head_mix, index * pairs),
    )
    packed = jnp.concatenate([part.reshape(-1) for part in small])
    packed = jnp.pad(packed, (0, -packed.shape[0] % 1024)).reshape(-1, LANES)
    packed = sum_all(packed).reshape(-1)
    sums = []
    first = 0
    for part in small:
        sums.append(packed[first : first + part.size].reshape(part.shape))
        first += part.size
    return (
        layer_output,
        input_grad,
        query_grad,
        key_grad,
        value_grad,
        out_weight_grad,
        gate_grad,
        up_grad,
        down_grad,
        *sums,
    )


def solution(mesh):
    placed = (
        P(("dp", "tensor"), None),
        P("dp", None),
        P("dp", "tensor"),
        P("dp", "tensor"),
        P("dp", "tensor"),
        P("tensor", "dp"),
        P("dp", "tensor"),
        P("dp", "tensor"),
        P("tensor", "dp"),
        P(),
        P(),
        P(),
        P(),
        P(),
        P(("dp", "tensor"), None),
    )
    return jax.shard_map(
        shards,
        mesh=mesh,
        in_specs=placed,
        out_specs=(
            P(("dp", "tensor"), None),
            P(("dp", "tensor"), None),
            P("dp", "tensor"),
            P("dp", "tensor"),
            P("dp", "tensor"),
            P("tensor", "dp"),
            P("dp", "tensor"),
            P("dp", "tensor"),
            P("tensor", "dp"),
            P(),
            P(),
            P(),
            P(),
            P(),
        ),
        check_vma=False,
    )
```
